128 devices in a mesh: row: 16 (over z, y), col: 8 (over x, core).
Axes of the slice: x: 4, y: 4, z: 4, core: 2. Of those that a mesh axis runs over, the one named last changes fastest.
Arguments:
- queries: bfloat16 [2048, 8192], P('row', 'col'), may hold values from -42 to 42
- new_keys: bfloat16 [2048, 1024], P('row', 'col'), may hold values from -12 to 12
- new_values: bfloat16 [2048, 1024], P('row', 'col'), may hold values from -8 to 8
- key_cache: bfloat16 [2048, 256, 1024], P('row', None, 'col'), may hold values from -4 to 4
- value_cache: bfloat16 [2048, 256, 1024], P('row', None, 'col'), may hold values from -4 to 4
- residual: bfloat16 [2048, 8192], P('row', 'col'), may hold values from -3 to 3
- out_weight: bfloat16 [8192, 8192], P('row', 'col'), may hold values from -0.0625 to 0.0625
- tenant: int32 [2048], P('row'), may hold values from 0 to 127, as said below
- tenant_slot_index: int32 [128], replicated, may hold values from 0 to 127, each once
- read_bank: bfloat16 [2, 128, 64, 8192], P(None, 'row', None, 'col'), may hold values from -0.0625 to 0.0625
- write_bank: bfloat16 [2, 128, 64, 8192], P(None, 'row', None, 'col'), may hold values from -0.375 to 0.375
- mean_bank: bfloat16 [2, 128, 8192], P(None, 'row', 'col'), may hold values from -1.25 to 1.25
Outputs:
- erased_out: bfloat16 [2048, 8192], P('row', 'col')
The draws below stay inside these ranges and needn't reach their ends.
Inputs may be any that keep to these rules, and one draw needn't show every extreme that they name: In each aligned block of 128 rows (the rows of one index of row) no tenant appears more than 3 times, and some tenant appears exactly 3 times in every block. `tenant_slot_index`: each bank slot belongs to exactly one tenant.
All inputs are finite; a program needn't handle non-finite values.
Results may differ from the reference program's by a relative error of at most 0.012.
Values may be sent and summed in bfloat16 or wider, within the bound.
No kernel may reach another device: no remote copies, remote signals or barrier semaphores. Data moves between devices by JAX's collectives and lax.ppermute only.
A program may use at most 128 MiB of HBM per device.

```python
import math
import jax
import jax.numpy as jnp
from jax import lax

D = 8192
HEADS = 64
KVH = 8
HD = 128
RANK = 64
MOST = 3
ROWS_DEV = 128
CTX = 256
BATCH = 2048
TEN = 128


def cache_keys(key):
    full_shape = (BATCH, CTX, KVH * HD)
    sub_key = jax.random.fold_in(key, 7)
    drawn = jnp.clip(jax.random.normal(sub_key, full_shape, jnp.float32), -4.0, 4.0)
    return drawn


def draw_key_cache(key, part):
    return cache_keys(key).astype(jnp.bfloat16)


def draw_queries(key, part):
    full_shape = (BATCH, HEADS * HD)
    sub_key = jax.random.fold_in(key, 13)
    drawn = jnp.clip(jax.random.normal(sub_key, full_shape, jnp.float32), -4.0, 4.0)
    return drawn.astype(jnp.bfloat16)


def draw_tenant(key, part):
    blocks = BATCH // ROWS_DEV
    busiest_tenant = jax.random.randint(jax.random.fold_in(key, 21), (), 0, TEN).astype(jnp.int32)
    popularity = jax.random.randint(jax.random.fold_in(key, 22), (TEN,), 0, 8).astype(jnp.int32)
    tokens = jnp.arange(TEN * MOST, dtype=jnp.int32)
    token_owner = tokens // MOST

    def one_block(block_key):
        jitter = jax.random.randint(jax.random.fold_in(block_key, 1), (TEN * MOST,), 0, 4096).astype(jnp.int32)
        priority = (popularity[token_owner] * 512 + jitter) * (TEN * MOST) + tokens
        priority = jnp.where(token_owner == busiest_tenant, -1, priority)
        top_values, picked = lax.top_k(priority, ROWS_DEV - MOST)
        chosen_ids = jnp.concatenate([jnp.full((MOST,), busiest_tenant, jnp.int32), token_owner[picked]])
        shuffle = jax.random.permutation(jax.random.fold_in(block_key, 2), ROWS_DEV)
        return chosen_ids[shuffle]
    block_keys = jax.random.split(jax.random.fold_in(key, 23), blocks)
    return jax.vmap(one_block)(block_keys).reshape(BATCH).astype(jnp.int32)


def block_levels(key, extent, cuts, low, largest):
    loudness = 1.0
    for dim, blocks in cuts:
        steps = jax.random.uniform(jax.random.fold_in(jax.random.fold_in(key, 6), dim), (blocks,), jnp.float32, low / len(cuts), largest / len(cuts))
        loudness = loudness * jnp.repeat(jnp.exp(steps), extent[dim] // blocks).reshape((-1,) + (1,) * (len(extent) - 1 - dim))
    return loudness


def gaussian(rng, shape, deviation, bound, cuts=(), held_as=jnp.bfloat16):
    level = block_levels(rng, shape, cuts, -0.22, 0.18) if cuts else 1.0
    values = jax.random.normal(rng, shape, jnp.float32) * deviation * level
    return jnp.minimum(jnp.maximum(values, -bound), bound).astype(held_as)


def setup_inputs(seed: int = 0) -> dict:
    seeds = jax.random.split(jax.random.key(seed), 13)
    return {
        "queries": draw_queries(jax.random.fold_in(seeds[12], 71), 0),
        "new_keys": gaussian(seeds[1], (BATCH, KVH * HD), 2.0, 12.0, ((0, 16), (1, 8))),
        "new_values": gaussian(seeds[2], (BATCH, KVH * HD), 1.5, 8.0, ((0, 16), (1, 8))),
        "key_cache": draw_key_cache(jax.random.fold_in(seeds[12], 71), 0),
        "value_cache": gaussian(seeds[4], (BATCH, CTX, KVH * HD), 1.0, 4.0, ((0, 16), (2, 8))),
        "residual": gaussian(seeds[5], (BATCH, D), 0.5, 3.0, ((0, 16), (1, 8))),
        "out_weight": gaussian(seeds[6], (HEADS * HD, D), (HEADS * HD) ** -0.5, 0.0625, ((0, 16), (1, 8))),
        "tenant": draw_tenant(jax.random.fold_in(seeds[12], 71), 0),
        "tenant_slot_index": jax.random.permutation(seeds[8], TEN).astype(jnp.int32),
        "read_bank": gaussian(seeds[9], (2, TEN, RANK, D), D ** -0.5, 0.0625, ((1, 16), (3, 8))),
        "write_bank": gaussian(seeds[10], (2, TEN, RANK, D), (4 * RANK) ** -0.5, 0.375, ((1, 16), (3, 8))),
        "mean_bank": gaussian(seeds[11], (2, TEN, D), 0.2, 1.25, ((1, 16), (2, 8))),
    }


def rounded(values):
    return lax.optimization_barrier(values.astype(jnp.bfloat16))

def attend_group(pieces):
    query_rows, fresh_keys, fresh_values, cached_keys, cached_values = pieces
    row_count = query_rows.shape[0]
    group_size = HEADS // KVH
    logit_scale = 1.0 / math.sqrt(HD)
    heads_of_query = query_rows.astype(jnp.float32).reshape(row_count, KVH, group_size, HD)
    past_keys = cached_keys.astype(jnp.float32).reshape(row_count, CTX, KVH, HD)
    past_values = cached_values.astype(jnp.float32).reshape(row_count, CTX, KVH, HD)
    current_keys = fresh_keys.astype(jnp.float32).reshape(row_count, KVH, HD)
    own_values = fresh_values.astype(jnp.float32).reshape(row_count, KVH, HD)
    past_scores = jnp.einsum('bkgd,blkd->bkgl', heads_of_query, past_keys) * logit_scale
    current_scores = jnp.einsum('qivl,qil->qiv', heads_of_query, current_keys) * logit_scale
    highest = jnp.maximum(lax.optimization_barrier(jnp.max(past_scores, axis=-1)), current_scores)
    past_exp = jnp.exp(past_scores - highest[..., None])
    own_exp = jnp.exp(current_scores - highest)
    denominator = lax.optimization_barrier(jnp.sum(past_exp, axis=-1)) + own_exp
    past_weights = rounded(past_exp / denominator[..., None])
    own_weights = rounded(own_exp / denominator)
    mixed_output = jnp.einsum('bkgl,blkd->bkgd', past_weights.astype(jnp.float32), past_values)
    mixed_output = mixed_output + own_weights.astype(jnp.float32)[..., None] * own_values[:, :, None, :]
    return mixed_output.reshape(row_count, HEADS * HD).astype(jnp.bfloat16)

def erase_rows(values, slot, reader, writer, centre):
    width = values.shape[1]

    def one_group(pieces):
        value_rows, slot_rows = pieces
        centered = rounded(value_rows.astype(jnp.float32) - centre[slot_rows].astype(jnp.float32))
        coefficients = jnp.einsum('gw,gkw->gk', centered.astype(jnp.float32), reader[slot_rows].astype(jnp.float32))
        coefficients = rounded(coefficients)
        deltas = jnp.einsum('gk,gkw->gw', coefficients.astype(jnp.float32), writer[slot_rows].astype(jnp.float32))
        deltas = rounded(deltas)
        return (value_rows.astype(jnp.float32) - deltas.astype(jnp.float32)).astype(jnp.bfloat16)
    grouped = lax.map(one_group, (values.reshape(-1, 8, width), slot.reshape(-1, 8)))
    return grouped.reshape(values.shape)

def reference(queries, new_keys, new_values, key_cache, value_cache, residual, out_weight, tenant, tenant_slot_index, read_bank, write_bank, mean_bank):
    slot = tenant_slot_index[tenant].astype(jnp.int32)
    groups = BATCH // 8
    attended = lax.map(attend_group, (queries.reshape(groups, 8, HEADS * HD), new_keys.reshape(groups, 8, KVH * HD), new_values.reshape(groups, 8, KVH * HD), key_cache.reshape(groups, 8, CTX, KVH * HD), value_cache.reshape(groups, 8, CTX, KVH * HD)))
    attended = attended.reshape(BATCH, HEADS * HD)
    cleaned = erase_rows(attended, slot, read_bank[0], write_bank[0], mean_bank[0])
    projected = jnp.dot(cleaned, out_weight, preferred_element_type=jnp.float32)
    hidden = (residual.astype(jnp.float32) + projected).astype(jnp.bfloat16)
    return erase_rows(hidden, slot, read_bank[1], write_bank[1], mean_bank[1])
```

```python
import functools
import math

import jax
import jax.numpy as jnp
from jax import lax
from jax.experimental import pallas as pl
from jax.experimental.pallas import tpu as pltpu
from jax.sharding import PartitionSpec as P

HEADS = 64
KVH = 8
HD = 128
MOST = 3
ROWS = 16
RING = 4
SLOTS = 8
RANK = 64
PART = SLOTS * MOST
PACKED = ROWS * PART
BLOCK = 128
WIDTH = 1024
QUARTER = WIDTH // RING

ALONG_Z = [[z * RING + y for z in range(RING)] for y in range(RING)]
ALONG_Y = [[z * RING + y for y in range(RING)] for z in range(RING)]
BF = jnp.bfloat16
F32 = jnp.float32


def whole(shape):
    return pl.BlockSpec(shape, lambda *_: (0,) * len(shape))


def params(mib):
    return pltpu.CompilerParams(vmem_limit_bytes=mib << 20)


def attention(queries, new_keys, new_values, key_cache, value_cache):
    row_count = queries.shape[0]
    kv_local = new_keys.shape[1] // HD
    group_size = HEADS // KVH
    history = key_cache.shape[1]
    logit_scale = 1.0 / math.sqrt(HD)
    heads_of_query = queries.reshape(row_count, kv_local, group_size, HD)
    past_keys = key_cache.reshape(row_count, history, kv_local, HD)
    past_values = value_cache.reshape(row_count, history, kv_local, HD)
    current_keys = new_keys.reshape(row_count, kv_local, HD)
    own_values = new_values.reshape(row_count, kv_local, HD)
    past_scores = (
        jnp.einsum("bkgd,blkd->bkgl", heads_of_query, past_keys, preferred_element_type=F32)
        * logit_scale
    )
    current_scores = (
        jnp.einsum("qivl,qil->qiv", heads_of_query, current_keys, preferred_element_type=F32)
        * logit_scale
    )
    highest = jnp.maximum(jnp.max(past_scores, axis=-1), current_scores)
    past_exp = jnp.exp(past_scores - highest[..., None])
    own_exp = jnp.exp(current_scores - highest)
    denominator = jnp.sum(past_exp, axis=-1) + own_exp
    past_weights = (past_exp / denominator[..., None]).astype(BF)
    own_weights = (own_exp / denominator).astype(BF)
    mixed = jnp.einsum("bkgl,blkd->bkgd", past_weights, past_values, preferred_element_type=F32)
    mixed = mixed + own_weights.astype(F32)[..., None] * own_values.astype(F32)[:, :, None, :]
    return mixed.reshape(row_count, kv_local * group_size * HD).astype(BF)


def packed_position(tenant, tenant_slot_index):
    tenants = jnp.arange(tenant_slot_index.shape[0], dtype=jnp.int32)
    slot = jnp.sum(
        jnp.where(tenant[:, None] == tenants[None, :], tenant_slot_index[None, :], 0), axis=1
    )
    order = jnp.arange(tenant.shape[0], dtype=jnp.int32)
    earlier = (tenant[:, None] == tenant[None, :]) & (order[None, :] < order[:, None])
    rank = jnp.sum(earlier.astype(jnp.int32), axis=1)
    return slot // SLOTS * PART + rank * SLOTS + slot % SLOTS


def slot_mask(rows):
    shape = (rows, SLOTS * RANK)
    return lax.broadcasted_iota(jnp.int32, shape, 0) % SLOTS == (
        lax.broadcasted_iota(jnp.int32, shape, 1) // RANK
    )


def coef_body(rows_ref, mean_ref, read_ref, out_ref):
    rows = rows_ref[...].astype(F32).reshape(PACKED // SLOTS, SLOTS, WIDTH)
    centered = (rows - mean_ref[...].astype(F32)).astype(BF).reshape(PACKED, WIDTH)
    full = lax.dot_general(
        centered, read_ref[...], (((1,), (1,)), ((), ())), preferred_element_type=F32
    )
    full = jnp.where(slot_mask(PACKED), full, 0.0)
    lanes = full[:, :128] + full[:, 128:256] + full[:, 256:384] + full[:, 384:]
    half = PACKED // 2
    out_ref[...] = lanes[:half] + pltpu.roll(lanes[half:], RANK, 1)


def partial_coefs(rows, mean_bank, read_bank, site):
    return pl.pallas_call(
        coef_body,
        grid=(1,),
        in_specs=[
            whole((PACKED, WIDTH)),
            pl.BlockSpec((None, SLOTS, WIDTH), lambda i: (site, 0, 0)),
            pl.BlockSpec((None, SLOTS * RANK, WIDTH), lambda i: (site, 0, 0)),
        ],
        out_specs=whole((PACKED // 2, 128)),
        out_shape=jax.ShapeDtypeStruct((PACKED // 2, 128), F32),
        compiler_params=params(32),
        cost_estimate=pl.CostEstimate(
            flops=2 * PACKED * WIDTH * SLOTS * RANK, bytes_accessed=2 << 20, transcendentals=0
        ),
        name="coefs",
    )(rows, mean_bank, read_bank.reshape(2, SLOTS * RANK, WIDTH))


def erased_rows(rows_ref, sum_ref, last_ref, write_ref):
    total = sum_ref[...] + last_ref[...].astype(F32)
    both = jnp.concatenate([total, pltpu.roll(total, RANK, 1)], axis=0)
    wide = jnp.concatenate([both] * (SLOTS * RANK // 128), axis=1)
    wide = jnp.where(slot_mask(PACKED), wide, 0.0).astype(BF)
    delta = jnp.dot(wide, write_ref[...], preferred_element_type=F32).astype(BF)
    return rows_ref[...].astype(F32) - delta.astype(F32)


def spread_body(rows_ref, sum_ref, last_ref, write_ref, out_ref):
    erased = erased_rows(rows_ref, sum_ref, last_ref, write_ref)
    for z in range(RING):
        for y in range(RING):
            first = QUARTER * quarter_of(y)
            pieces = []
            for step in range(RING):
                start = PART * (z * RING + (y + step) % RING)
                pieces.append(erased[start : start + PART, first : first + QUARTER])
            out_ref[z * RING + y] = jnp.concatenate(pieces, axis=0).astype(BF)


def home_body(rows_ref, sum_ref, last_ref, write_ref, out_ref):
    out_ref[...] = erased_rows(rows_ref, sum_ref, last_ref, write_ref).astype(BF)


def apply_eraser(body, rows, summed, last, write_bank, site, shape):
    return pl.pallas_call(
        body,
        grid=(1,),
        in_specs=[
            whole((PACKED, WIDTH)),
            whole((PACKED // 2, 128)),
            whole((PACKED // 2, 128)),
            pl.BlockSpec((None, SLOTS * RANK, WIDTH), lambda i: (site, 0, 0)),
        ],
        out_specs=whole(shape),
        out_shape=jax.ShapeDtypeStruct(shape, BF),
        compiler_params=params(32),
        cost_estimate=pl.CostEstimate(
            flops=2 * PACKED * WIDTH * SLOTS * RANK, bytes_accessed=3 << 20, transcendentals=0
        ),
        name="erase",
    )(rows, summed, last, write_bank.reshape(2, SLOTS * RANK, WIDTH))


def quarter_of(y):
    return 2 * (y % 2) + y // 2


def along_col(values, move):
    return lax.ppermute(values, "col", [(i, move(i)) for i in range(8)])


def along_y(values, step):
    return lax.ppermute(
        values, "row", [(i, i // RING * RING + (i + step) % RING) for i in range(ROWS)]
    )


def sum_but_last(partial):
    for bit in (1, 2):
        partial = partial + along_col(partial.astype(BF), lambda i: i ^ bit).astype(F32)
    return partial, along_col(partial.astype(BF), lambda i: i ^ 4)


def compact_body(y_ref, target_ref, rows_ref, out_ref):
    rows = rows_ref[...].astype(F32)
    for step in range(RING):
        target = target_ref[pl.ds((y_ref[0] + step) % RING, 1), :]
        table = (lax.broadcasted_iota(jnp.int32, (PACKED, BLOCK), 0) == target).astype(BF)
        part = rows[:, PART * step : PART * (step + 1), :].reshape(PACKED, QUARTER).astype(BF)
        picked = lax.dot_general(
            table, part, (((0,), (0,)), ((), ())), preferred_element_type=F32
        )
        out_ref[BLOCK * step : BLOCK * (step + 1), :] = picked.astype(BF)


def compact(y, targets, rows):
    return pl.pallas_call(
        compact_body,
        grid_spec=pltpu.PrefetchScalarGridSpec(
            num_scalar_prefetch=1,
            grid=(1,),
            in_specs=[whole((RING, BLOCK)), whole((ROWS, RING * PART, QUARTER))],
            out_specs=whole((RING * BLOCK, QUARTER)),
        ),
        out_shape=jax.ShapeDtypeStruct((RING * BLOCK, QUARTER), BF),
        compiler_params=params(32),
        cost_estimate=pl.CostEstimate(
            flops=2 * RING * BLOCK * PACKED * QUARTER, bytes_accessed=1 << 20, transcendentals=0
        ),
        name="compact",
    )(y, targets, rows)


def project_body(scalar_ref, *refs):
    same, other = refs[0:4], refs[4:8]
    kept_ref, swapped_ref, own_ref, up_ref, far_ref, down_ref, sum_ref = refs[8:]
    step = pl.program_id(0)
    for which in range(RING):

        @pl.when(step == which)
        def _():
            a, b = same[which][...], other[which][...]
            straight = scalar_ref[RING] == 0
            first, second = jnp.where(straight, a, b), jnp.where(straight, b, a)
            product = jnp.dot(first, kept_ref[...], preferred_element_type=F32)
            product += jnp.dot(second, swapped_ref[...], preferred_element_type=F32)
            if which == 0:
                sum_ref[...] = product
            elif which < RING - 1:
                sum_ref[...] += product
            else:
                product += sum_ref[...]
                own_ref[...] = product[:BLOCK]
                up_ref[...] = product[BLOCK : 2 * BLOCK].astype(BF)
                far_ref[...] = product[2 * BLOCK : 3 * BLOCK].astype(BF)
                down_ref[...] = product[3 * BLOCK :].astype(BF)


def project(scalars, same, other, kept, swapped):
    act = whole((RING * BLOCK, QUARTER))
    weight = pl.BlockSpec((None, QUARTER, WIDTH), lambda i, s: (s[i], 0, 0))
    out = whole((BLOCK, WIDTH))
    sent = jax.ShapeDtypeStruct((BLOCK, WIDTH), BF)
    return pl.pallas_call(
        project_body,
        grid_spec=pltpu.PrefetchScalarGridSpec(
            num_scalar_prefetch=1,
            grid=(RING,),
            in_specs=[act] * 8 + [weight] * 2,
            out_specs=[out] * 4,
            scratch_shapes=[pltpu.VMEM((RING * BLOCK, WIDTH), F32)],
        ),
        out_shape=[jax.ShapeDtypeStruct((BLOCK, WIDTH), F32), sent, sent, sent],
        compiler_params=params(40),
        cost_estimate=pl.CostEstimate(
            flops=2 * RING * BLOCK * 8 * QUARTER * WIDTH, bytes_accessed=7 << 20, transcendentals=0
        ),
        name="project",
    )(scalars, *same, *other, kept, swapped)


def local(
    queries,
    new_keys,
    new_values,
    key_cache,
    value_cache,
    residual,
    out_weight,
    tenant,
    tenant_slot_index,
    read_bank,
    write_bank,
    mean_bank,
):
    row, col = lax.axis_index("row"), lax.axis_index("col")
    y = row % RING
    upper = y // 2
    half = out_weight.shape[0] // 2
    kept = lax.dynamic_slice_in_dim(out_weight, upper * half, half)
    swapped = lax.dynamic_slice_in_dim(out_weight, (1 - upper) * half, half)
    swapped = lax.ppermute(swapped, "row", [(i, i ^ 2) for i in range(ROWS)])
    kept = lax.all_gather(kept, "row", axis_index_groups=ALONG_Z)
    swapped = lax.all_gather(swapped, "row", axis_index_groups=ALONG_Z)

    target = packed_position(tenant, tenant_slot_index)
    targets = lax.all_gather(target, "row", axis_index_groups=ALONG_Y)
    table = (jnp.arange(PACKED, dtype=jnp.int32)[:, None] == target[None, :]).astype(BF)

    def dispatch(values):
        packed = jnp.dot(table, values, preferred_element_type=F32).astype(BF)
        packed = packed.reshape(ROWS, PART, WIDTH)
        return lax.all_to_all(packed, "row", 0, 0, tiled=True).reshape(PACKED, WIDTH)

    attended = attention(queries, new_keys, new_values, key_cache, value_cache)
    rows = dispatch(attended)
    summed, last = sum_but_last(partial_coefs(rows, mean_bank, read_bank, 0))
    cleaned = apply_eraser(
        spread_body, rows, summed, last, write_bank, 0, (ROWS, RING * PART, QUARTER)
    )
    cleaned = lax.all_to_all(cleaned, "row", 0, 0, tiled=True)
    here = compact(y[None], targets, cleaned)

    after = along_col(here, lambda i: (i + 2) % 8)
    before = along_col(here, lambda i: (i - 2) % 8)
    across = along_col(here, lambda i: (i + 4) % 8)
    same = [here, after, before, across]
    other = [along_col(part, lambda i: i ^ 1) for part in same]
    x = col // 2
    scalars = jnp.stack([x, (x + 3) % RING, (x + 1) % RING, (x + 2) % RING, (col % 2) ^ upper])
    own, up, far, down = project(scalars.astype(jnp.int32), same, other, kept, swapped)
    projected = own + along_y(up, 1).astype(F32) + along_y(down, 3).astype(F32)
    projected = projected + along_y(far, 2).astype(F32)
    hidden = (residual.astype(F32) + projected).astype(BF)

    rows = dispatch(hidden)
    summed, last = sum_but_last(partial_coefs(rows, mean_bank, read_bank, 1))
    erased = apply_eraser(home_body, rows, summed, last, write_bank, 1, (PACKED, WIDTH))
    erased = lax.all_to_all(erased.reshape(ROWS, PART, WIDTH), "row", 0, 0, tiled=True)
    return lax.dot_general(
        table,
        erased.reshape(PACKED, WIDTH),
        (((0,), (0,)), ((), ())),
        preferred_element_type=F32,
    ).astype(BF)


def solution(mesh):
    return jax.shard_map(
        local,
        mesh=mesh,
        in_specs=(
            P("row", "col"),
            P("row", "col"),
            P("row", "col"),
            P("row", None, "col"),
            P("row", None, "col"),
            P("row", "col"),
            P("row", "col"),
            P("row"),
            P(),
            P(None, "row", None, "col"),
            P(None, "row", None, "col"),
            P(None, "row", "col"),
        ),
        out_specs=P("row", "col"),
        check_vma=False,
    )
```

```python
import functools
import math

import jax
import jax.numpy as jnp
from jax import lax
from jax.experimental import pallas as pl
from jax.experimental.pallas import tpu as pltpu
from jax.sharding import PartitionSpec as P

HEADS = 64
KVH = 8
HD = 128
MOST = 3
ROWS = 16
RING = 4
SLOTS = 8
RANK = 64
PART = SLOTS * MOST
PACKED = ROWS * PART
BLOCK = 128
TILE = 512
CHUNK = 32
WIDTH = 1024
QUARTER = WIDTH // RING

ALONG_Z = [[z * RING + y for z in range(RING)] for y in range(RING)]
ALONG_Y = [[z * RING + y for y in range(RING)] for z in range(RING)]
BF = jnp.bfloat16
F32 = jnp.float32


def whole(shape):
    return pl.BlockSpec(shape, lambda *_: (0,) * len(shape))


def params(mib):
    return pltpu.CompilerParams(vmem_limit_bytes=mib << 20)


def in_hbm(*arrays):
    return [pltpu.with_memory_space_constraint(array, pltpu.HBM) for array in arrays]


def attend_body(
    q_ref, key_ref, value_ref, target_ref, keys_ref, values_ref,
    out_ref, after_ref, heads_ref, mix_ref, all_ref
):
    step = pl.program_id(0)
    group = HEADS // KVH
    scale = 1.0 / math.sqrt(HD)
    q = q_ref[...].astype(F32)
    for head in range(group):
        heads_ref[pl.ds(head, CHUNK, stride=group), :] = q[:, HD * head : HD * (head + 1)]
    heads = heads_ref[...].reshape(CHUNK, group, HD)
    past = scale * jnp.einsum(
        "bhd,bld->bhl", heads.astype(BF), keys_ref[...], preferred_element_type=F32
    )
    key = key_ref[...].astype(F32)[:, None, :]
    own = scale * jnp.sum(heads * key, axis=-1, keepdims=True)
    top = jnp.maximum(jnp.max(past, axis=-1, keepdims=True), own)
    past, own = jnp.exp(past - top), jnp.exp(own - top)
    inverse = 1.0 / (jnp.sum(past, axis=-1, keepdims=True) + own)
    weights = (past * inverse).astype(BF)
    own = (own * inverse).astype(BF).astype(F32)
    mixed = jnp.einsum("bhl,bld->bhd", weights, values_ref[...], preferred_element_type=F32)
    mixed = mixed + own * value_ref[...].astype(F32)[:, None, :]
    mix_ref[...] = mixed.reshape(CHUNK * group, HD)
    rows = pl.ds(pl.multiple_of(step * CHUNK, CHUNK), CHUNK)
    for head in range(group):
        picked = mix_ref[pl.ds(head, CHUNK, stride=group), :]
        all_ref[rows, HD * head : HD * (head + 1)] = picked.astype(BF)

    @pl.when(step == pl.num_programs(0) - 1)
    def _():
        table = (
            lax.broadcasted_iota(jnp.int32, (PACKED, BLOCK), 0) == target_ref[...]
        ).astype(BF)
        packed = jnp.dot(table, all_ref[...], preferred_element_type=F32)
        out_ref[...] = packed.astype(BF)
        after_ref[...] = target_ref[...]


def attend_and_pack(queries, new_keys, new_values, key_cache, value_cache, target):
    history = key_cache.shape[1]
    group = HEADS // KVH
    by_row = lambda *tail: pl.BlockSpec((CHUNK,) + tail, lambda i: (i,) + (0,) * len(tail))
    queries, new_keys, new_values, key_cache, value_cache = in_hbm(
        queries, new_keys, new_values, key_cache, value_cache
    )
    return pl.pallas_call(
        attend_body,
        grid=(BLOCK // CHUNK,),
        in_specs=[
            by_row(WIDTH),
            by_row(HD),
            by_row(HD),
            whole((1, BLOCK)),
            by_row(history, HD),
            by_row(history, HD),
        ],
        out_specs=[whole((PACKED, WIDTH)), whole((1, BLOCK))],
        out_shape=[
            jax.ShapeDtypeStruct((PACKED, WIDTH), BF),
            jax.ShapeDtypeStruct((1, BLOCK), jnp.int32),
        ],
        scratch_shapes=[
            pltpu.VMEM((CHUNK * group, HD), F32),
            pltpu.VMEM((CHUNK * group, HD), F32),
            pltpu.VMEM((BLOCK, WIDTH), BF),
        ],
        compiler_params=params(20),
        cost_estimate=pl.CostEstimate(
            flops=4 * BLOCK * history * WIDTH, bytes_accessed=17 << 20, transcendentals=0
        ),
        name="attend",
    )(queries, new_keys, new_values, target, key_cache, value_cache)


def packed_position(tenant, tenant_slot_index):
    tenants = jnp.arange(tenant_slot_index.shape[0], dtype=jnp.int32)
    slot = jnp.sum(
        jnp.where(tenant[:, None] == tenants[None, :], tenant_slot_index[None, :], 0), axis=1
    )
    order = jnp.arange(tenant.shape[0], dtype=jnp.int32)
    earlier = (tenant[:, None] == tenant[None, :]) & (order[None, :] < order[:, None])
    rank = jnp.sum(earlier.astype(jnp.int32), axis=1)
    return slot // SLOTS * PART + rank * SLOTS + slot % SLOTS


def slot_mask(rows):
    shape = (rows, SLOTS * RANK)
    return lax.broadcasted_iota(jnp.int32, shape, 0) % SLOTS == (
        lax.broadcasted_iota(jnp.int32, shape, 1) // RANK
    )


def coef_body(rows_ref, mean_ref, read_ref, out_ref, short_ref):
    rows = rows_ref[...].astype(F32).reshape(PACKED // SLOTS, SLOTS, WIDTH)
    centered = (rows - mean_ref[...].astype(F32)).astype(BF).reshape(PACKED, WIDTH)
    full = lax.dot_general(
        centered, read_ref[...], (((1,), (1,)), ((), ())), preferred_element_type=F32
    )
    full = jnp.where(slot_mask(PACKED), full, 0.0)
    lanes = full[:, :128] + full[:, 128:256] + full[:, 256:384] + full[:, 384:]
    half = PACKED // 2
    packed = lanes[:half] + pltpu.roll(lanes[half:], RANK, 1)
    out_ref[...] = packed
    short_ref[...] = packed.astype(BF)


def partial_coefs(rows, mean_bank, read_bank, site):
    return pl.pallas_call(
        coef_body,
        grid=(1,),
        in_specs=[
            whole((PACKED, WIDTH)),
            pl.BlockSpec((None, SLOTS, WIDTH), lambda i: (site, 0, 0)),
            pl.BlockSpec((None, SLOTS * RANK, WIDTH), lambda i: (site, 0, 0)),
        ],
        out_specs=[whole((PACKED // 2, 128))] * 2,
        out_shape=[jax.ShapeDtypeStruct((PACKED // 2, 128), kind) for kind in (F32, BF)],
        compiler_params=params(16),
        cost_estimate=pl.CostEstimate(
            flops=2 * PACKED * WIDTH * SLOTS * RANK, bytes_accessed=2 << 20, transcendentals=0
        ),
        name="coefs",
    )(rows, mean_bank, read_bank.reshape(2, SLOTS * RANK, WIDTH))


def erased_rows(rows_ref, sum_ref, last_ref, write_ref):
    total = sum_ref[...] + last_ref[...].astype(F32)
    both = jnp.concatenate([total, pltpu.roll(total, RANK, 1)], axis=0)
    wide = jnp.concatenate([both] * (SLOTS * RANK // 128), axis=1)
    wide = jnp.where(slot_mask(PACKED), wide, 0.0).astype(BF)
    delta = jnp.dot(wide, write_ref[...], preferred_element_type=F32).astype(BF)
    return rows_ref[...].astype(F32) - delta.astype(F32)


def spread_body(core_ref, rows_ref, sum_ref, last_ref, write_ref, out_ref):
    erased = erased_rows(rows_ref, sum_ref, last_ref, write_ref).astype(BF).astype(F32)
    first_core = core_ref[0] == 0
    for y in range(RING):
        start = QUARTER * 2 * (y % 2)
        low = erased[:, start : start + QUARTER]
        high = erased[:, start + QUARTER : start + 2 * QUARTER]
        part = jnp.where(first_core, low, high) if y < 2 else jnp.where(first_core, high, low)
        for z in range(RING):
            pieces = []
            for step in range(RING):
                start = PART * (z * RING + (y + step) % RING)
                pieces.append(part[start : start + PART])
            out_ref[z * RING + y] = jnp.concatenate(pieces, axis=0).astype(BF)


def home_body(rows_ref, sum_ref, last_ref, write_ref, out_ref):
    out_ref[...] = erased_rows(rows_ref, sum_ref, last_ref, write_ref).astype(BF)


def apply_eraser(body, rows, summed, last, write_bank, site, shape, extra=()):
    write_bank = write_bank.reshape(2, SLOTS * RANK, WIDTH)
    if site == 0:
        write_bank = in_hbm(write_bank)[0]
    return pl.pallas_call(
        body,
        grid=(1,),
        in_specs=[pl.BlockSpec(memory_space=pltpu.SMEM)] * len(extra)
        + [
            whole((PACKED, WIDTH)),
            whole((PACKED // 2, 128)),
            whole((PACKED // 2, 128)),
            pl.BlockSpec((None, SLOTS * RANK, WIDTH), lambda i: (site, 0, 0)),
        ],
        out_specs=whole(shape),
        out_shape=jax.ShapeDtypeStruct(shape, BF),
        compiler_params=params(16),
        cost_estimate=pl.CostEstimate(
            flops=2 * PACKED * WIDTH * SLOTS * RANK, bytes_accessed=3 << 20, transcendentals=0
        ),
        name="erase",
    )(*extra, rows, summed, last, write_bank)


def along_col(values, move):
    return lax.ppermute(values, "col", [(i, move(i)) for i in range(8)])


def along_y(values, step):
    return lax.ppermute(
        values, "row", [(i, i // RING * RING + (i + step) % RING) for i in range(ROWS)]
    )


def sum_but_last(partial, short):
    for bit in (1, 2):
        partial = partial + along_col(short, lambda i: i ^ bit).astype(F32)
        short = partial.astype(BF)
    return partial, along_col(short, lambda i: i ^ 4)


def compact_body(y_ref, target_ref, rows_ref, out_ref):
    rows = rows_ref[...].astype(F32)
    for step in range(RING):
        target = target_ref[pl.ds((y_ref[0] + step) & 3, 1), :]
        table = (lax.broadcasted_iota(jnp.int32, (PACKED, BLOCK), 0) == target).astype(BF)
        part = rows[:, PART * step : PART * (step + 1), :].reshape(PACKED, QUARTER).astype(BF)
        picked = lax.dot_general(
            table, part, (((0,), (0,)), ((), ())), preferred_element_type=F32
        )
        out_ref[BLOCK * step : BLOCK * (step + 1), :] = picked.astype(BF)


def compact(y, targets, rows):
    return pl.pallas_call(
        compact_body,
        grid_spec=pltpu.PrefetchScalarGridSpec(
            num_scalar_prefetch=1,
            grid=(1,),
            in_specs=[whole((RING, BLOCK)), whole((ROWS, RING * PART, QUARTER))],
            out_specs=whole((RING * BLOCK, QUARTER)),
        ),
        out_shape=jax.ShapeDtypeStruct((RING * BLOCK, QUARTER), BF),
        compiler_params=params(16),
        cost_estimate=pl.CostEstimate(
            flops=2 * RING * BLOCK * PACKED * QUARTER, bytes_accessed=1 << 20, transcendentals=0
        ),
        name="compact",
    )(y, targets, rows)


def project_body(scalar_ref, *refs):
    same, other = refs[0:RING], refs[RING : 2 * RING]
    weight_ref, far_ref, up_ref, down_ref, own_ref = refs[2 * RING :]
    near = pl.multiple_of(scalar_ref[1] * QUARTER, QUARTER)
    away = pl.multiple_of(QUARTER - near, QUARTER)
    product = jnp.zeros((RING * BLOCK, TILE), F32)
    for step, offset in enumerate((0, 3, 1, 2)):
        z = (scalar_ref[0] + offset) & 3
        product += jnp.dot(
            same[step][...], weight_ref[z, pl.ds(near, QUARTER), :], preferred_element_type=F32
        )
        product += jnp.dot(
            other[step][...], weight_ref[z, pl.ds(away, QUARTER), :], preferred_element_type=F32
        )
    own_ref[...] = product[:BLOCK]
    up_ref[...] = product[BLOCK : 2 * BLOCK].astype(BF)
    far_ref[...] = product[2 * BLOCK : 3 * BLOCK].astype(BF)
    down_ref[...] = product[3 * BLOCK :].astype(BF)


def project(scalars, same, other, weight):
    act = whole((RING * BLOCK, QUARTER))
    out = pl.BlockSpec((BLOCK, TILE), lambda i, s: (0, i))
    sent = jax.ShapeDtypeStruct((BLOCK, WIDTH), BF)
    return pl.pallas_call(
        project_body,
        grid_spec=pltpu.PrefetchScalarGridSpec(
            num_scalar_prefetch=1,
            grid=(WIDTH // TILE,),
            in_specs=[act] * 8
            + [pl.BlockSpec((RING, 2 * QUARTER, TILE), lambda i, s: (0, 0, i))],
            out_specs=[out] * 4,
        ),
        out_shape=[sent, sent, sent, jax.ShapeDtypeStruct((BLOCK, WIDTH), F32)],
        compiler_params=params(20),
        cost_estimate=pl.CostEstimate(
            flops=2 * RING * BLOCK * 8 * QUARTER * WIDTH, bytes_accessed=7 << 20, transcendentals=0
        ),
        name="project",
    )(scalars, *same, *other, *in_hbm(weight))


def local(
    queries,
    new_keys,
    new_values,
    key_cache,
    value_cache,
    residual,
    out_weight,
    tenant,
    tenant_slot_index,
    read_bank,
    write_bank,
    mean_bank,
):
    row, col = lax.axis_index("row"), lax.axis_index("col")
    x, core, y, upper = col >> 1, col & 1, row & 3, (row & 3) >> 1
    half = out_weight.shape[0] // 2
    swapped = lax.ppermute(out_weight[half:], "row", [(i, i ^ 2) for i in range(ROWS)])
    target = packed_position(tenant, tenant_slot_index)

    def dispatch(packed):
        packed = packed.reshape(ROWS, PART, WIDTH)
        return lax.all_to_all(packed, "row", 0, 0, tiled=True).reshape(PACKED, WIDTH)

    packed, target = attend_and_pack(
        queries, new_keys, new_values, key_cache, value_cache, target[None]
    )
    swapped, target = lax.optimization_barrier((swapped, target))
    weight = jnp.concatenate([out_weight[:half], swapped], axis=0)
    weight = lax.all_gather(weight, "row", axis_index_groups=ALONG_Z)
    rows = dispatch(packed)
    targets = lax.all_gather(target[0], "row", axis_index_groups=ALONG_Y)
    table = (jnp.arange(PACKED, dtype=jnp.int32)[:, None] == target).astype(BF)
    summed, last = sum_but_last(*partial_coefs(rows, mean_bank, read_bank, 0))
    shape = (ROWS, RING * PART, QUARTER)
    cleaned = apply_eraser(spread_body, rows, summed, last, write_bank, 0, shape, (core[None],))
    cleaned = lax.all_to_all(cleaned, "row", 0, 0, tiled=True)
    here = compact(y[None], targets, cleaned)

    after = along_col(here, lambda i: (i + 2) % 8)
    before = along_col(here, lambda i: (i - 2) % 8)
    across = along_col(here, lambda i: (i + 4) % 8)
    same = [here, after, before, across]
    other = [along_col(part, lambda i: i ^ 1) for part in same]
    place = jnp.stack([x, core ^ upper])
    far, up, down, own = project(place, same, other, weight)
    far, up, down = along_y(far, 2), along_y(up, 1), along_y(down, 3)
    projected = own + up.astype(F32) + down.astype(F32) + far.astype(F32)
    hidden = (residual.astype(F32) + projected).astype(BF)

    rows = dispatch(jnp.dot(table, hidden, preferred_element_type=F32).astype(BF))
    summed, last = sum_but_last(*partial_coefs(rows, mean_bank, read_bank, 1))
    erased = apply_eraser(home_body, rows, summed, last, write_bank, 1, (PACKED, WIDTH))
    erased = lax.all_to_all(erased.reshape(ROWS, PART, WIDTH), "row", 0, 0, tiled=True)
    return lax.dot_general(
        table,
        erased.reshape(PACKED, WIDTH),
        (((0,), (0,)), ((), ())),
        preferred_element_type=F32,
    ).astype(BF)


def solution(mesh):
    return jax.shard_map(
        local,
        mesh=mesh,
        in_specs=(
            P("row", "col"),
            P("row", "col"),
            P("row", "col"),
            P("row", None, "col"),
            P("row", None, "col"),
            P("row", "col"),
            P("row", "col"),
            P("row"),
            P(),
            P(None, "row", None, "col"),
            P(None, "row", None, "col"),
            P(None, "row", "col"),
        ),
        out_specs=P("row", "col"),
        check_vma=False,
    )
```

```python
import functools
import math

import jax
import jax.numpy as jnp
from jax import lax
from jax.experimental import pallas as pl
from jax.experimental.pallas import tpu as pltpu
from jax.sharding import PartitionSpec as P

HEADS = 64
KVH = 8
HD = 128
MOST = 3
ROWS = 16
COLS = 8
RING = 4
AROUND = (0, 3, 1, 2)
SLOTS = 8
RANK = 64
PART = SLOTS * MOST
PACKED = ROWS * PART
BLOCK = 128
TILE = 512
CHUNK = 32
WIDTH = 1024
QUARTER = WIDTH // RING

BF = jnp.bfloat16
F32 = jnp.float32


def whole(shape):
    return pl.BlockSpec(shape, lambda *_: (0,) * len(shape))


def params(mib):
    return pltpu.CompilerParams(vmem_limit_bytes=mib << 20)


def in_hbm(*arrays):
    return [pltpu.with_memory_space_constraint(array, pltpu.HBM) for array in arrays]


def attend_body(
    q_ref, key_ref, value_ref, target_ref, keys_ref, values_ref,
    out_ref, after_ref, heads_ref, mix_ref, all_ref
):
    step = pl.program_id(0)
    group = HEADS // KVH
    scale = 1.0 / math.sqrt(HD)
    q = q_ref[...].astype(F32)
    for head in range(group):
        heads_ref[pl.ds(head, CHUNK, stride=group), :] = q[:, HD * head : HD * (head + 1)]
    heads = heads_ref[...].reshape(CHUNK, group, HD)
    past = scale * jnp.einsum(
        "bhd,bld->bhl", heads.astype(BF), keys_ref[...], preferred_element_type=F32
    )
    key = key_ref[...].astype(F32)[:, None, :]
    own = scale * jnp.sum(heads * key, axis=-1, keepdims=True)
    top = jnp.maximum(jnp.max(past, axis=-1, keepdims=True), own)
    past, own = jnp.exp(past - top), jnp.exp(own - top)
    inverse = 1.0 / (jnp.sum(past, axis=-1, keepdims=True) + own)
    weights = (past * inverse).astype(BF)
    own = (own * inverse).astype(BF).astype(F32)
    mixed = jnp.einsum("bhl,bld->bhd", weights, values_ref[...], preferred_element_type=F32)
    mixed = mixed + own * value_ref[...].astype(F32)[:, None, :]
    mix_ref[...] = mixed.reshape(CHUNK * group, HD)
    rows = pl.ds(pl.multiple_of(step * CHUNK, CHUNK), CHUNK)
    for head in range(group):
        picked = mix_ref[pl.ds(head, CHUNK, stride=group), :]
        all_ref[rows, HD * head : HD * (head + 1)] = picked.astype(BF)

    @pl.when(step == pl.num_programs(0) - 1)
    def _():
        table = (
            lax.broadcasted_iota(jnp.int32, (PACKED, BLOCK), 0) == target_ref[...]
        ).astype(BF)
        packed = jnp.dot(table, all_ref[...], preferred_element_type=F32)
        out_ref[...] = packed.astype(BF)
        after_ref[...] = target_ref[...]


def attend_and_pack(queries, new_keys, new_values, key_cache, value_cache, target):
    history = key_cache.shape[1]
    group = HEADS // KVH
    by_row = lambda *tail: pl.BlockSpec((CHUNK,) + tail, lambda i: (i,) + (0,) * len(tail))
    queries, new_keys, new_values, key_cache, value_cache = in_hbm(
        queries, new_keys, new_values, key_cache, value_cache
    )
    return pl.pallas_call(
        attend_body,
        grid=(BLOCK // CHUNK,),
        in_specs=[
            by_row(WIDTH),
            by_row(HD),
            by_row(HD),
            whole((1, BLOCK)),
            by_row(history, HD),
            by_row(history, HD),
        ],
        out_specs=[whole((PACKED, WIDTH)), whole((1, BLOCK))],
        out_shape=[
            jax.ShapeDtypeStruct((PACKED, WIDTH), BF),
            jax.ShapeDtypeStruct((1, BLOCK), jnp.int32),
        ],
        scratch_shapes=[
            pltpu.VMEM((CHUNK * group, HD), F32),
            pltpu.VMEM((CHUNK * group, HD), F32),
            pltpu.VMEM((BLOCK, WIDTH), BF),
        ],
        compiler_params=params(20),
        cost_estimate=pl.CostEstimate(
            flops=4 * BLOCK * history * WIDTH, bytes_accessed=17 << 20, transcendentals=0
        ),
        name="attend",
    )(queries, new_keys, new_values, target, key_cache, value_cache)


def packed_position(tenant, tenant_slot_index):
    tenants = jnp.arange(tenant_slot_index.shape[0], dtype=jnp.int32)
    slot = jnp.sum(
        jnp.where(tenant[:, None] == tenants[None, :], tenant_slot_index[None, :], 0), axis=1
    )
    order = jnp.arange(tenant.shape[0], dtype=jnp.int32)
    earlier = (tenant[:, None] == tenant[None, :]) & (order[None, :] < order[:, None])
    rank = jnp.sum(earlier.astype(jnp.int32), axis=1)
    return slot // SLOTS * PART + rank * SLOTS + slot % SLOTS


def slot_mask(rows):
    shape = (rows, SLOTS * RANK)
    return lax.broadcasted_iota(jnp.int32, shape, 0) % SLOTS == (
        lax.broadcasted_iota(jnp.int32, shape, 1) // RANK
    )


def coef_body(rows_ref, mean_ref, read_ref, out_ref, short_ref):
    rows = rows_ref[...].astype(F32).reshape(PACKED // SLOTS, SLOTS, WIDTH)
    centered = (rows - mean_ref[...].astype(F32)).astype(BF).reshape(PACKED, WIDTH)
    full = lax.dot_general(
        centered, read_ref[...], (((1,), (1,)), ((), ())), preferred_element_type=F32
    )
    full = jnp.where(slot_mask(PACKED), full, 0.0)
    lanes = full[:, :128] + full[:, 128:256] + full[:, 256:384] + full[:, 384:]
    half = PACKED // 2
    packed = lanes[:half] + pltpu.roll(lanes[half:], RANK, 1)
    out_ref[...] = packed
    short_ref[...] = packed.astype(BF)


def partial_coefs(rows, mean_bank, read_bank, site):
    return pl.pallas_call(
        coef_body,
        grid=(1,),
        in_specs=[
            whole((PACKED, WIDTH)),
            pl.BlockSpec((None, SLOTS, WIDTH), lambda i: (site, 0, 0)),
            pl.BlockSpec((None, SLOTS * RANK, WIDTH), lambda i: (site, 0, 0)),
        ],
        out_specs=[whole((PACKED // 2, 128))] * 2,
        out_shape=[jax.ShapeDtypeStruct((PACKED // 2, 128), kind) for kind in (F32, BF)],
        compiler_params=params(16),
        cost_estimate=pl.CostEstimate(
            flops=2 * PACKED * WIDTH * SLOTS * RANK, bytes_accessed=2 << 20, transcendentals=0
        ),
        name="coefs",
    )(rows, mean_bank, read_bank.reshape(2, SLOTS * RANK, WIDTH))


def erased_rows(rows_ref, sum_ref, sum1_ref, sum2_ref, sum3_ref, write_ref):
    total = sum_ref[...] + sum1_ref[...].astype(F32)
    total = total + sum2_ref[...].astype(F32) + sum3_ref[...].astype(F32)
    both = jnp.concatenate([total, pltpu.roll(total, RANK, 1)], axis=0)
    wide = jnp.concatenate([both] * (SLOTS * RANK // 128), axis=1)
    wide = jnp.where(slot_mask(PACKED), wide, 0.0).astype(BF)
    delta = jnp.dot(wide, write_ref[...], preferred_element_type=F32).astype(BF)
    return rows_ref[...].astype(F32) - delta.astype(F32)


def spread_body(core_ref, rows_ref, sum_ref, sum1_ref, sum2_ref, sum3_ref, write_ref, out_ref):
    erased = erased_rows(rows_ref, sum_ref, sum1_ref, sum2_ref, sum3_ref, write_ref).astype(BF).astype(F32)
    first_core = core_ref[0] == 0
    for y in range(RING):
        start = QUARTER * 2 * (y % 2)
        low = erased[:, start : start + QUARTER]
        high = erased[:, start + QUARTER : start + 2 * QUARTER]
        part = jnp.where(first_core, low, high) if y < 2 else jnp.where(first_core, high, low)
        for z in range(RING):
            pieces = []
            for step in range(RING):
                start = PART * (z * RING + (y + step) % RING)
                pieces.append(part[start : start + PART])
            out_ref[z * RING + y] = jnp.concatenate(pieces, axis=0).astype(BF)


def home_body(rows_ref, sum_ref, sum1_ref, sum2_ref, sum3_ref, write_ref, out_ref):
    out_ref[...] = erased_rows(rows_ref, sum_ref, sum1_ref, sum2_ref, sum3_ref, write_ref).astype(BF)


def apply_eraser(body, rows, summed, others, write_bank, site, shape, extra=()):
    write_bank = write_bank.reshape(2, SLOTS * RANK, WIDTH)
    if site == 0:
        write_bank = in_hbm(write_bank)[0]
    return pl.pallas_call(
        body,
        grid=(1,),
        in_specs=[pl.BlockSpec(memory_space=pltpu.SMEM)] * len(extra)
        + [
            whole((PACKED, WIDTH)),
            *[whole((PACKED // 2, 128))] * RING,
            pl.BlockSpec((None, SLOTS * RANK, WIDTH), lambda i: (site, 0, 0)),
        ],
        out_specs=whole(shape),
        out_shape=jax.ShapeDtypeStruct(shape, BF),
        compiler_params=params(16),
        cost_estimate=pl.CostEstimate(
            flops=2 * PACKED * WIDTH * SLOTS * RANK, bytes_accessed=3 << 20, transcendentals=0
        ),
        name="erase",
    )(*extra, rows, summed, *others, write_bank)


def along_col(values, move):
    return lax.ppermute(values, "col", [(i, move(i)) for i in range(8)])


def along_y(values, step):
    return lax.ppermute(
        values, "row", [(i, i // RING * RING + (i + step) % RING) for i in range(ROWS)]
    )


def along_z(values, step):
    return lax.ppermute(values, "row", [(i, (i + RING * step) % ROWS) for i in range(ROWS)])


def gather_sums(partial, short):
    partial = partial + along_col(short, lambda i: i ^ 1).astype(F32)
    short = partial.astype(BF)
    return partial, [along_col(short, lambda i, by=by: (i + by) % COLS) for by in (4, 2, 6)]


def compact_body(*refs):
    targets, rows_ref, out_ref = refs[:RING], refs[RING], refs[RING + 1]
    rows = rows_ref[...].astype(F32)
    for step in range(RING):
        table = (
            lax.broadcasted_iota(jnp.int32, (PACKED, BLOCK), 0) == targets[step][...]
        ).astype(BF)
        part = rows[:, PART * step : PART * (step + 1), :].reshape(PACKED, QUARTER).astype(BF)
        picked = lax.dot_general(
            table, part, (((0,), (0,)), ((), ())), preferred_element_type=F32
        )
        out_ref[BLOCK * step : BLOCK * (step + 1), :] = picked.astype(BF)


def compact(targets, rows):
    return pl.pallas_call(
        compact_body,
        grid=(1,),
        in_specs=[whole((1, BLOCK))] * RING + [whole((ROWS, RING * PART, QUARTER))],
        out_specs=whole((RING * BLOCK, QUARTER)),
        out_shape=jax.ShapeDtypeStruct((RING * BLOCK, QUARTER), BF),
        compiler_params=params(16),
        cost_estimate=pl.CostEstimate(
            flops=2 * RING * BLOCK * PACKED * QUARTER, bytes_accessed=1 << 20, transcendentals=0
        ),
        name="compact",
    )(*targets, rows)


def project_body(place_ref, *refs):
    same, other = refs[0:RING], refs[RING : 2 * RING]
    kept, swapped = refs[2 * RING : 3 * RING], refs[3 * RING : 4 * RING]
    far_ref, up_ref, down_ref, own_ref, weight_ref, sems = refs[4 * RING :]
    x, near, z = place_ref[0], place_ref[1], place_ref[2]
    copies = {}
    for step, offset in enumerate(AROUND):
        block = (z + offset) & 3
        for which, source in enumerate((kept[step], swapped[step])):
            copies[step, which] = pltpu.make_async_copy(
                source.at[pl.ds(0, QUARTER), :],
                weight_ref.at[block, pl.ds(which * QUARTER, QUARTER), :],
                sems.at[step, which],
            )
            copies[step, which].start()
    for copy in copies.values():
        copy.wait()
    near = pl.multiple_of(near * QUARTER, QUARTER)
    away = pl.multiple_of(QUARTER - near, QUARTER)
    for tile in range(0, WIDTH, TILE):
        columns = pl.ds(tile, TILE)
        product = jnp.zeros((RING * BLOCK, TILE), F32)
        for step, offset in enumerate(AROUND):
            block = (x + offset) & 3
            product += jnp.dot(
                same[step][...],
                weight_ref[block, pl.ds(near, QUARTER), columns],
                preferred_element_type=F32,
            )
            product += jnp.dot(
                other[step][...],
                weight_ref[block, pl.ds(away, QUARTER), columns],
                preferred_element_type=F32,
            )
        own_ref[:, columns] = product[:BLOCK]
        up_ref[:, columns] = product[BLOCK : 2 * BLOCK].astype(BF)
        far_ref[:, columns] = product[2 * BLOCK : 3 * BLOCK].astype(BF)
        down_ref[:, columns] = product[3 * BLOCK :].astype(BF)


def project(place, same, other, kept, swapped):
    out = whole((BLOCK, WIDTH))
    sent = jax.ShapeDtypeStruct((BLOCK, WIDTH), BF)
    return pl.pallas_call(
        project_body,
        grid=(1,),
        in_specs=[pl.BlockSpec(memory_space=pltpu.SMEM)]
        + [whole((RING * BLOCK, QUARTER))] * 8
        + [pl.BlockSpec(memory_space=pltpu.HBM)] * 8,
        out_specs=[out] * 4,
        out_shape=[sent, sent, sent, jax.ShapeDtypeStruct((BLOCK, WIDTH), F32)],
        scratch_shapes=[
            pltpu.VMEM((RING, 2 * QUARTER, WIDTH), BF),
            pltpu.SemaphoreType.DMA((RING, 2)),
        ],
        compiler_params=params(20),
        cost_estimate=pl.CostEstimate(
            flops=2 * RING * BLOCK * 8 * QUARTER * WIDTH, bytes_accessed=7 << 20, transcendentals=0
        ),
        name="project",
    )(place, *in_hbm(*same, *other, *kept, *swapped))


def local(
    queries,
    new_keys,
    new_values,
    key_cache,
    value_cache,
    residual,
    out_weight,
    tenant,
    tenant_slot_index,
    read_bank,
    write_bank,
    mean_bank,
):
    row, col = lax.axis_index("row"), lax.axis_index("col")
    x, core, y, z = col >> 1, col & 1, row & 3, row >> 2
    half = out_weight.shape[0] // 2
    kept0 = out_weight[:half]
    swapped0 = lax.ppermute(out_weight[half:], "row", [(i, i ^ 2) for i in range(ROWS)])
    kept1, kept2 = along_z(kept0, 1), along_z(kept0, 3)
    target = packed_position(tenant, tenant_slot_index)

    def dispatch(packed):
        packed = packed.reshape(ROWS, PART, WIDTH)
        return lax.all_to_all(packed, "row", 0, 0, tiled=True).reshape(PACKED, WIDTH)

    packed, target = attend_and_pack(
        queries, new_keys, new_values, key_cache, value_cache, target[None]
    )
    targets = [target] + [along_y(target, by) for by in (3, 2, 1)]
    swapped0, kept1, kept2, packed = lax.optimization_barrier((swapped0, kept1, kept2, packed))
    rows = dispatch(packed)
    table = (jnp.arange(PACKED, dtype=jnp.int32)[:, None] == target).astype(BF)
    partial, short = partial_coefs(rows, mean_bank, read_bank, 0)
    swapped0, short = lax.optimization_barrier((swapped0, short))
    swapped1, swapped2 = along_z(swapped0, 1), along_z(swapped0, 3)
    summed, others = gather_sums(partial, short)
    shape = (ROWS, RING * PART, QUARTER)
    cleaned = apply_eraser(spread_body, rows, summed, others, write_bank, 0, shape, (core[None],))
    swapped1, swapped2, cleaned = lax.optimization_barrier((swapped1, swapped2, cleaned))
    cleaned = lax.all_to_all(cleaned, "row", 0, 0, tiled=True)
    kept1, swapped2, cleaned = lax.optimization_barrier((kept1, swapped2, cleaned))
    kept3, swapped3 = along_z(kept1, 1), along_z(swapped2, 3)
    here = compact(targets, cleaned)

    after = along_col(here, lambda i: (i + 2) % 8)
    before = along_col(here, lambda i: (i - 2) % 8)
    across = along_col(here, lambda i: (i + 4) % 8)
    same = [here, after, before, across]
    other = [along_col(part, lambda i: i ^ 1) for part in same]
    place = jnp.stack([x, core ^ (y >> 1), z])
    kept, swapped = [out_weight, kept1, kept2, kept3], [swapped0, swapped1, swapped2, swapped3]
    far, up, down, own = project(place, same, other, kept, swapped)
    far, up, down = along_y(far, 2), along_y(up, 1), along_y(down, 3)
    projected = own + up.astype(F32) + down.astype(F32) + far.astype(F32)
    hidden = (residual.astype(F32) + projected).astype(BF)

    rows = dispatch(jnp.dot(table, hidden, preferred_element_type=F32).astype(BF))
    summed, others = gather_sums(*partial_coefs(rows, mean_bank, read_bank, 1))
    erased = apply_eraser(home_body, rows, summed, others, write_bank, 1, (PACKED, WIDTH))
    erased = lax.all_to_all(erased.reshape(ROWS, PART, WIDTH), "row", 0, 0, tiled=True)
    return lax.dot_general(
        table,
        erased.reshape(PACKED, WIDTH),
        (((0,), (0,)), ((), ())),
        preferred_element_type=F32,
    ).astype(BF)


def solution(mesh):
    return jax.shard_map(
        local,
        mesh=mesh,
        in_specs=(
            P("row", "col"),
            P("row", "col"),
            P("row", "col"),
            P("row", None, "col"),
            P("row", None, "col"),
            P("row", "col"),
            P("row", "col"),
            P("row"),
            P(),
            P(None, "row", None, "col"),
            P(None, "row", None, "col"),
            P(None, "row", "col"),
        ),
        out_specs=P("row", "col"),
        check_vma=False,
    )
```

```python
import functools
import math

import jax
import jax.numpy as jnp
from jax import lax
from jax.experimental import pallas as pl
from jax.experimental.pallas import tpu as pltpu
from jax.sharding import PartitionSpec as P

HEADS = 64
KVH = 8
HD = 128
MOST = 3
ROWS = 16
COLS = 8
RING = 4
AROUND = (0, 3, 1, 2)
SLOTS = 8
RANK = 64
PART = SLOTS * MOST
PACKED = ROWS * PART
BLOCK = 128
TILE = 512
CHUNK = 32
WIDTH = 1024
QUARTER = WIDTH // RING

BF = jnp.bfloat16
F32 = jnp.float32


def whole(shape):
    return pl.BlockSpec(shape, lambda *_: (0,) * len(shape))


def params(mib):
    return pltpu.CompilerParams(vmem_limit_bytes=mib << 20)


def in_hbm(*arrays):
    return [pltpu.with_memory_space_constraint(array, pltpu.HBM) for array in arrays]


def attend_body(
    q_ref, key_ref, value_ref, target_ref, keys_ref, values_ref,
    out_ref, after_ref, heads_ref, mix_ref, all_ref
):
    step = pl.program_id(0)
    group = HEADS // KVH
    scale = 1.0 / math.sqrt(HD)
    q = q_ref[...].astype(F32)
    for head in range(group):
        heads_ref[pl.ds(head, CHUNK, stride=group), :] = q[:, HD * head : HD * (head + 1)]
    heads = heads_ref[...].reshape(CHUNK, group, HD)
    past = scale * jnp.einsum(
        "bhd,bld->bhl", heads.astype(BF), keys_ref[...], preferred_element_type=F32
    )
    key = key_ref[...].astype(F32)[:, None, :]
    own = scale * jnp.sum(heads * key, axis=-1, keepdims=True)
    top = jnp.maximum(jnp.max(past, axis=-1, keepdims=True), own)
    past, own = jnp.exp(past - top), jnp.exp(own - top)
    inverse = 1.0 / (jnp.sum(past, axis=-1, keepdims=True) + own)
    weights = (past * inverse).astype(BF)
    own = (own * inverse).astype(BF).astype(F32)
    mixed = jnp.einsum("bhl,bld->bhd", weights, values_ref[...], preferred_element_type=F32)
    mixed = mixed + own * value_ref[...].astype(F32)[:, None, :]
    mix_ref[...] = mixed.reshape(CHUNK * group, HD)
    rows = pl.ds(pl.multiple_of(step * CHUNK, CHUNK), CHUNK)
    for head in range(group):
        picked = mix_ref[pl.ds(head, CHUNK, stride=group), :]
        all_ref[rows, HD * head : HD * (head + 1)] = picked.astype(BF)

    @pl.when(step == pl.num_programs(0) - 1)
    def _():
        table = (
            lax.broadcasted_iota(jnp.int32, (PACKED, BLOCK), 0) == target_ref[...]
        ).astype(BF)
        packed = jnp.dot(table, all_ref[...], preferred_element_type=F32)
        out_ref[...] = packed.astype(BF)
        after_ref[...] = target_ref[...]


def attend_and_pack(queries, new_keys, new_values, key_cache, value_cache, target):
    history = key_cache.shape[1]
    group = HEADS // KVH
    by_row = lambda *tail: pl.BlockSpec((CHUNK,) + tail, lambda i: (i,) + (0,) * len(tail))
    queries, new_keys, new_values, key_cache, value_cache = in_hbm(
        queries, new_keys, new_values, key_cache, value_cache
    )
    return pl.pallas_call(
        attend_body,
        grid=(BLOCK // CHUNK,),
        in_specs=[
            by_row(WIDTH),
            by_row(HD),
            by_row(HD),
            whole((1, BLOCK)),
            by_row(history, HD),
            by_row(history, HD),
        ],
        out_specs=[whole((PACKED, WIDTH)), whole((1, BLOCK))],
        out_shape=[
            jax.ShapeDtypeStruct((PACKED, WIDTH), BF),
            jax.ShapeDtypeStruct((1, BLOCK), jnp.int32),
        ],
        scratch_shapes=[
            pltpu.VMEM((CHUNK * group, HD), F32),
            pltpu.VMEM((CHUNK * group, HD), F32),
            pltpu.VMEM((BLOCK, WIDTH), BF),
        ],
        compiler_params=params(20),
        cost_estimate=pl.CostEstimate(
            flops=4 * BLOCK * history * WIDTH, bytes_accessed=17 << 20, transcendentals=0
        ),
        name="attend",
    )(queries, new_keys, new_values, target, key_cache, value_cache)


def packed_position(tenant, tenant_slot_index):
    tenants = jnp.arange(tenant_slot_index.shape[0], dtype=jnp.int32)
    slot = jnp.sum(
        jnp.where(tenant[:, None] == tenants[None, :], tenant_slot_index[None, :], 0), axis=1
    )
    order = jnp.arange(tenant.shape[0], dtype=jnp.int32)
    earlier = (tenant[:, None] == tenant[None, :]) & (order[None, :] < order[:, None])
    rank = jnp.sum(earlier.astype(jnp.int32), axis=1)
    return slot // SLOTS * PART + rank * SLOTS + slot % SLOTS


def slot_mask(rows):
    shape = (rows, SLOTS * RANK)
    return lax.broadcasted_iota(jnp.int32, shape, 0) % SLOTS == (
        lax.broadcasted_iota(jnp.int32, shape, 1) // RANK
    )


def coef_body(rows_ref, mean_ref, read_ref, out_ref, short_ref):
    rows = rows_ref[...].astype(F32).reshape(PACKED // SLOTS, SLOTS, WIDTH)
    centered = (rows - mean_ref[...].astype(F32)).astype(BF).reshape(PACKED, WIDTH)
    full = lax.dot_general(
        centered, read_ref[...], (((1,), (1,)), ((), ())), preferred_element_type=F32
    )
    full = jnp.where(slot_mask(PACKED), full, 0.0)
    lanes = full[:, :128] + full[:, 128:256] + full[:, 256:384] + full[:, 384:]
    half = PACKED // 2
    packed = lanes[:half] + pltpu.roll(lanes[half:], RANK, 1)
    out_ref[...] = packed
    short_ref[...] = packed.astype(BF)


def partial_coefs(rows, mean_bank, read_bank, site):
    return pl.pallas_call(
        coef_body,
        grid=(1,),
        in_specs=[
            whole((PACKED, WIDTH)),
            pl.BlockSpec((None, SLOTS, WIDTH), lambda i: (site, 0, 0)),
            pl.BlockSpec((None, SLOTS * RANK, WIDTH), lambda i: (site, 0, 0)),
        ],
        out_specs=[whole((PACKED // 2, 128))] * 2,
        out_shape=[jax.ShapeDtypeStruct((PACKED // 2, 128), kind) for kind in (F32, BF)],
        compiler_params=params(16),
        cost_estimate=pl.CostEstimate(
            flops=2 * PACKED * WIDTH * SLOTS * RANK, bytes_accessed=2 << 20, transcendentals=0
        ),
        name="coefs",
    )(rows, mean_bank, read_bank.reshape(2, SLOTS * RANK, WIDTH))


def erased_rows(rows_ref, sum_ref, sum1_ref, sum2_ref, sum3_ref, write_ref):
    total = sum_ref[...] + sum1_ref[...].astype(F32)
    total = total + sum2_ref[...].astype(F32) + sum3_ref[...].astype(F32)
    both = jnp.concatenate([total, pltpu.roll(total, RANK, 1)], axis=0)
    wide = jnp.concatenate([both] * (SLOTS * RANK // 128), axis=1)
    wide = jnp.where(slot_mask(PACKED), wide, 0.0).astype(BF)
    delta = jnp.dot(wide, write_ref[...], preferred_element_type=F32).astype(BF)
    return rows_ref[...].astype(F32) - delta.astype(F32)


def spread_body(core_ref, rows_ref, sum_ref, sum1_ref, sum2_ref, sum3_ref, write_ref, out_ref):
    erased = erased_rows(rows_ref, sum_ref, sum1_ref, sum2_ref, sum3_ref, write_ref).astype(BF).astype(F32)
    first_core = core_ref[0] == 0
    for y in range(RING):
        start = QUARTER * 2 * (y % 2)
        low = erased[:, start : start + QUARTER]
        high = erased[:, start + QUARTER : start + 2 * QUARTER]
        part = jnp.where(first_core, low, high) if y < 2 else jnp.where(first_core, high, low)
        for z in range(RING):
            pieces = []
            for step in range(RING):
                start = PART * (z * RING + (y + step) % RING)
                pieces.append(part[start : start + PART])
            out_ref[z * RING + y] = jnp.concatenate(pieces, axis=0).astype(BF)


def home_body(rows_ref, sum_ref, sum1_ref, sum2_ref, sum3_ref, write_ref, out_ref):
    out_ref[...] = erased_rows(rows_ref, sum_ref, sum1_ref, sum2_ref, sum3_ref, write_ref).astype(BF)


def apply_eraser(body, rows, summed, others, write_bank, site, shape, extra=()):
    write_bank = write_bank.reshape(2, SLOTS * RANK, WIDTH)
    if site == 0:
        write_bank = in_hbm(write_bank)[0]
    return pl.pallas_call(
        body,
        grid=(1,),
        in_specs=[pl.BlockSpec(memory_space=pltpu.SMEM)] * len(extra)
        + [
            whole((PACKED, WIDTH)),
            *[whole((PACKED // 2, 128))] * RING,
            pl.BlockSpec((None, SLOTS * RANK, WIDTH), lambda i: (site, 0, 0)),
        ],
        out_specs=whole(shape),
        out_shape=jax.ShapeDtypeStruct(shape, BF),
        compiler_params=params(16),
        cost_estimate=pl.CostEstimate(
            flops=2 * PACKED * WIDTH * SLOTS * RANK, bytes_accessed=3 << 20, transcendentals=0
        ),
        name="erase",
    )(*extra, rows, summed, *others, write_bank)


def along_col(values, move):
    return lax.ppermute(values, "col", [(i, move(i)) for i in range(8)])


def along_y(values, step):
    return lax.ppermute(
        values, "row", [(i, i // RING * RING + (i + step) % RING) for i in range(ROWS)]
    )


def along_z(values, step):
    return lax.ppermute(values, "row", [(i, (i + RING * step) % ROWS) for i in range(ROWS)])


def gather_sums(partial, short):
    partial = partial + along_col(short, lambda i: i ^ 1).astype(F32)
    short = partial.astype(BF)
    return partial, [along_col(short, lambda i, by=by: (i + by) % COLS) for by in (2, 6, 4)]


def compact_body(*refs):
    targets, rows_ref, out_ref = refs[:RING], refs[RING], refs[RING + 1]
    rows = rows_ref[...].astype(F32)
    for step in range(RING):
        table = (
            lax.broadcasted_iota(jnp.int32, (PACKED, BLOCK), 0) == targets[step][...]
        ).astype(BF)
        part = rows[:, PART * step : PART * (step + 1), :].reshape(PACKED, QUARTER).astype(BF)
        picked = lax.dot_general(
            table, part, (((0,), (0,)), ((), ())), preferred_element_type=F32
        )
        out_ref[BLOCK * step : BLOCK * (step + 1), :] = picked.astype(BF)


def compact(targets, rows):
    return pl.pallas_call(
        compact_body,
        grid=(1,),
        in_specs=[whole((1, BLOCK))] * RING + [whole((ROWS, RING * PART, QUARTER))],
        out_specs=whole((RING * BLOCK, QUARTER)),
        out_shape=jax.ShapeDtypeStruct((RING * BLOCK, QUARTER), BF),
        compiler_params=params(16),
        cost_estimate=pl.CostEstimate(
            flops=2 * RING * BLOCK * PACKED * QUARTER, bytes_accessed=1 << 20, transcendentals=0
        ),
        name="compact",
    )(*targets, rows)


def project_body(place_ref, *refs):
    same, other = refs[0:RING], refs[RING : 2 * RING]
    kept, swapped = refs[2 * RING : 3 * RING], refs[3 * RING : 4 * RING]
    far_ref, up_ref, down_ref, own_ref, weight_ref, sems = refs[4 * RING :]
    x, near, z = place_ref[0], place_ref[1], place_ref[2]

    def load(step, which, block):
        source = (kept, swapped)[which][step]
        return pltpu.make_async_copy(
            source.at[pl.ds(0, QUARTER), :],
            weight_ref.at[block, pl.ds(which * QUARTER, QUARTER), :],
            sems.at[block, which],
        )

    for step, offset in enumerate(AROUND):
        for which in range(2):
            load(step, which, (z + offset) & 3).start()
    near = pl.multiple_of(near * QUARTER, QUARTER)
    away = pl.multiple_of(QUARTER - near, QUARTER)
    for tile in range(0, WIDTH, TILE):
        columns = pl.ds(tile, TILE)
        product = jnp.zeros((RING * BLOCK, TILE), F32)
        for step, offset in enumerate(AROUND):
            block = (x + offset) & 3
            if tile == 0:
                for which in range(2):
                    load(step, which, block).wait()
            product += jnp.dot(
                same[step][...],
                weight_ref[block, pl.ds(near, QUARTER), columns],
                preferred_element_type=F32,
            )
            product += jnp.dot(
                other[step][...],
                weight_ref[block, pl.ds(away, QUARTER), columns],
                preferred_element_type=F32,
            )
        own_ref[:, columns] = product[:BLOCK]
        up_ref[:, columns] = product[BLOCK : 2 * BLOCK].astype(BF)
        far_ref[:, columns] = product[2 * BLOCK : 3 * BLOCK].astype(BF)
        down_ref[:, columns] = product[3 * BLOCK :].astype(BF)


def project(place, same, other, kept, swapped):
    out = whole((BLOCK, WIDTH))
    sent = jax.ShapeDtypeStruct((BLOCK, WIDTH), BF)
    return pl.pallas_call(
        project_body,
        grid=(1,),
        in_specs=[pl.BlockSpec(memory_space=pltpu.SMEM)]
        + [whole((RING * BLOCK, QUARTER))] * 8
        + ([pl.BlockSpec(memory_space=pltpu.HBM)] * 3 + [pl.BlockSpec(memory_space=pl.ANY)]) * 2,
        out_specs=[out] * 4,
        out_shape=[sent, sent, sent, jax.ShapeDtypeStruct((BLOCK, WIDTH), F32)],
        scratch_shapes=[
            pltpu.VMEM((RING, 2 * QUARTER, WIDTH), BF),
            pltpu.SemaphoreType.DMA((RING, 2)),
        ],
        compiler_params=params(20),
        cost_estimate=pl.CostEstimate(
            flops=2 * RING * BLOCK * 8 * QUARTER * WIDTH, bytes_accessed=7 << 20, transcendentals=0
        ),
        name="project",
    )(place, *in_hbm(*same, *other, *kept[:3]), kept[3], *in_hbm(*swapped[:3]), swapped[3])


def local(
    queries,
    new_keys,
    new_values,
    key_cache,
    value_cache,
    residual,
    out_weight,
    tenant,
    tenant_slot_index,
    read_bank,
    write_bank,
    mean_bank,
):
    row, col = lax.axis_index("row"), lax.axis_index("col")
    x, core, y, z = col >> 1, col & 1, row & 3, row >> 2
    half = out_weight.shape[0] // 2
    kept0 = out_weight[:half]
    swapped0 = lax.ppermute(out_weight[half:], "row", [(i, i ^ 2) for i in range(ROWS)])
    kept1, kept2 = along_z(kept0, 1), along_z(kept0, 3)
    target = packed_position(tenant, tenant_slot_index)

    def dispatch(packed):
        packed = packed.reshape(ROWS, PART, WIDTH)
        return lax.all_to_all(packed, "row", 0, 0, tiled=True).reshape(PACKED, WIDTH)

    packed, target = attend_and_pack(
        queries, new_keys, new_values, key_cache, value_cache, target[None]
    )
    targets = [target] + [along_y(target, by) for by in (3, 2, 1)]
    swapped0, kept1, kept2, packed = lax.optimization_barrier((swapped0, kept1, kept2, packed))
    rows = dispatch(packed)
    table = (jnp.arange(PACKED, dtype=jnp.int32)[:, None] == target).astype(BF)
    partial, short = partial_coefs(rows, mean_bank, read_bank, 0)
    swapped0, short = lax.optimization_barrier((swapped0, short))
    swapped1, swapped2 = along_z(swapped0, 1), along_z(swapped0, 3)
    summed, others = gather_sums(partial, short)
    shape = (ROWS, RING * PART, QUARTER)
    cleaned = apply_eraser(spread_body, rows, summed, others, write_bank, 0, shape, (core[None],))
    swapped1, swapped2, cleaned = lax.optimization_barrier((swapped1, swapped2, cleaned))
    cleaned = lax.all_to_all(cleaned, "row", 0, 0, tiled=True)
    kept1, swapped2, cleaned = lax.optimization_barrier((kept1, swapped2, cleaned))
    kept3, swapped3 = along_z(kept1, 1), along_z(swapped2, 3)
    here = compact(targets, cleaned)

    after = along_col(here, lambda i: (i + 2) % 8)
    before = along_col(here, lambda i: (i - 2) % 8)
    across = along_col(here, lambda i: (i + 4) % 8)
    same = [here, after, before, across]
    other = [along_col(part, lambda i: i ^ 1) for part in same]
    place = jnp.stack([x, core ^ (y >> 1), z])
    kept, swapped = [out_weight, kept1, kept2, kept3], [swapped0, swapped1, swapped2, swapped3]
    far, up, down, own = project(place, same, other, kept, swapped)
    far, up, down = along_y(far, 2), along_y(up, 1), along_y(down, 3)
    projected = own + up.astype(F32) + down.astype(F32) + far.astype(F32)
    hidden = (residual.astype(F32) + projected).astype(BF)

    rows = dispatch(jnp.dot(table, hidden, preferred_element_type=F32).astype(BF))
    summed, others = gather_sums(*partial_coefs(rows, mean_bank, read_bank, 1))
    erased = apply_eraser(home_body, rows, summed, others, write_bank, 1, (PACKED, WIDTH))
    erased = lax.all_to_all(erased.reshape(ROWS, PART, WIDTH), "row", 0, 0, tiled=True)
    return lax.dot_general(
        table,
        erased.reshape(PACKED, WIDTH),
        (((0,), (0,)), ((), ())),
        preferred_element_type=F32,
    ).astype(BF)


def solution(mesh):
    return jax.shard_map(
        local,
        mesh=mesh,
        in_specs=(
            P("row", "col"),
            P("row", "col"),
            P("row", "col"),
            P("row", None, "col"),
            P("row", None, "col"),
            P("row", "col"),
            P("row", "col"),
            P("row"),
            P(),
            P(None, "row", None, "col"),
            P(None, "row", None, "col"),
            P(None, "row", "col"),
        ),
        out_specs=P("row", "col"),
        check_vma=False,
    )
```

```python
import functools
import math

import jax
import jax.numpy as jnp
from jax import lax
from jax.experimental import pallas as pl
from jax.experimental.pallas import tpu as pltpu
from jax.sharding import PartitionSpec as P

HEADS = 64
KVH = 8
HD = 128
MOST = 3
ROWS = 16
COLS = 8
RING = 4
AROUND = (0, 3, 1, 2)
SLOTS = 8
RANK = 64
PART = SLOTS * MOST
PACKED = ROWS * PART
BLOCK = 128
TILE = 512
CHUNK = 32
WIDTH = 1024
QUARTER = WIDTH // RING

BF = jnp.bfloat16
F32 = jnp.float32


def whole(shape):
    return pl.BlockSpec(shape, lambda *_: (0,) * len(shape))


def params(mib):
    return pltpu.CompilerParams(vmem_limit_bytes=mib << 20)


def in_hbm(*arrays):
    return [pltpu.with_memory_space_constraint(array, pltpu.HBM) for array in arrays]


def attend_body(
    q_ref, key_ref, value_ref, target_ref, keys_ref, values_ref,
    out_ref, after_ref, heads_ref, mix_ref, all_ref
):
    step = pl.program_id(0)
    group = HEADS // KVH
    scale = 1.0 / math.sqrt(HD)
    q = q_ref[...].astype(F32)
    for head in range(group):
        heads_ref[pl.ds(head, CHUNK, stride=group), :] = q[:, HD * head : HD * (head + 1)]
    heads = heads_ref[...].reshape(CHUNK, group, HD)
    past = scale * jnp.einsum(
        "bhd,bld->bhl", heads.astype(BF), keys_ref[...], preferred_element_type=F32
    )
    key = key_ref[...].astype(F32)[:, None, :]
    own = scale * jnp.sum(heads * key, axis=-1, keepdims=True)
    top = jnp.maximum(jnp.max(past, axis=-1, keepdims=True), own)
    past, own = jnp.exp(past - top), jnp.exp(own - top)
    inverse = 1.0 / (jnp.sum(past, axis=-1, keepdims=True) + own)
    weights = (past * inverse).astype(BF)
    own = (own * inverse).astype(BF).astype(F32)
    mixed = jnp.einsum("bhl,bld->bhd", weights, values_ref[...], preferred_element_type=F32)
    mixed = mixed + own * value_ref[...].astype(F32)[:, None, :]
    mix_ref[...] = mixed.reshape(CHUNK * group, HD)
    rows = pl.ds(pl.multiple_of(step * CHUNK, CHUNK), CHUNK)
    for head in range(group):
        picked = mix_ref[pl.ds(head, CHUNK, stride=group), :]
        all_ref[rows, HD * head : HD * (head + 1)] = picked.astype(BF)

    @pl.when(step == pl.num_programs(0) - 1)
    def _():
        table = (
            lax.broadcasted_iota(jnp.int32, (PACKED, BLOCK), 0) == target_ref[...]
        ).astype(BF)
        packed = jnp.dot(table, all_ref[...], preferred_element_type=F32)
        out_ref[...] = packed.astype(BF)
        after_ref[...] = target_ref[...]


def attend_and_pack(queries, new_keys, new_values, key_cache, value_cache, target):
    history = key_cache.shape[1]
    group = HEADS // KVH
    by_row = lambda *tail: pl.BlockSpec((CHUNK,) + tail, lambda i: (i,) + (0,) * len(tail))
    queries, new_keys, new_values, key_cache, value_cache = in_hbm(
        queries, new_keys, new_values, key_cache, value_cache
    )
    return pl.pallas_call(
        attend_body,
        grid=(BLOCK // CHUNK,),
        in_specs=[
            by_row(WIDTH),
            by_row(HD),
            by_row(HD),
            whole((1, BLOCK)),
            by_row(history, HD),
            by_row(history, HD),
        ],
        out_specs=[whole((PACKED, WIDTH)), whole((1, BLOCK))],
        out_shape=[
            jax.ShapeDtypeStruct((PACKED, WIDTH), BF),
            jax.ShapeDtypeStruct((1, BLOCK), jnp.int32),
        ],
        scratch_shapes=[
            pltpu.VMEM((CHUNK * group, HD), F32),
            pltpu.VMEM((CHUNK * group, HD), F32),
            pltpu.VMEM((BLOCK, WIDTH), BF),
        ],
        compiler_params=params(20),
        cost_estimate=pl.CostEstimate(
            flops=4 * BLOCK * history * WIDTH, bytes_accessed=17 << 20, transcendentals=0
        ),
        name="attend",
    )(queries, new_keys, new_values, target, key_cache, value_cache)


def packed_position(tenant, tenant_slot_index):
    tenants = jnp.arange(tenant_slot_index.shape[0], dtype=jnp.int32)
    slot = jnp.sum(
        jnp.where(tenant[:, None] == tenants[None, :], tenant_slot_index[None, :], 0), axis=1
    )
    order = jnp.arange(tenant.shape[0], dtype=jnp.int32)
    earlier = (tenant[:, None] == tenant[None, :]) & (order[None, :] < order[:, None])
    rank = jnp.sum(earlier.astype(jnp.int32), axis=1)
    return slot // SLOTS * PART + rank * SLOTS + slot % SLOTS


def slot_mask(rows):
    shape = (rows, SLOTS * RANK)
    return lax.broadcasted_iota(jnp.int32, shape, 0) % SLOTS == (
        lax.broadcasted_iota(jnp.int32, shape, 1) // RANK
    )


def coef_body(rows_ref, mean_ref, read_ref, out_ref, short_ref):
    rows = rows_ref[...].astype(F32).reshape(PACKED // SLOTS, SLOTS, WIDTH)
    centered = (rows - mean_ref[...].astype(F32)).astype(BF).reshape(PACKED, WIDTH)
    full = lax.dot_general(
        centered, read_ref[...], (((1,), (1,)), ((), ())), preferred_element_type=F32
    )
    full = jnp.where(slot_mask(PACKED), full, 0.0)
    lanes = full[:, :128] + full[:, 128:256] + full[:, 256:384] + full[:, 384:]
    half = PACKED // 2
    packed = lanes[:half] + pltpu.roll(lanes[half:], RANK, 1)
    out_ref[...] = packed
    short_ref[...] = packed.astype(BF)


def partial_coefs(rows, mean_bank, read_bank, site):
    return pl.pallas_call(
        coef_body,
        grid=(1,),
        in_specs=[
            whole((PACKED, WIDTH)),
            pl.BlockSpec((None, SLOTS, WIDTH), lambda i: (site, 0, 0)),
            pl.BlockSpec((None, SLOTS * RANK, WIDTH), lambda i: (site, 0, 0)),
        ],
        out_specs=[whole((PACKED // 2, 128))] * 2,
        out_shape=[jax.ShapeDtypeStruct((PACKED // 2, 128), kind) for kind in (F32, BF)],
        compiler_params=params(16),
        cost_estimate=pl.CostEstimate(
            flops=2 * PACKED * WIDTH * SLOTS * RANK, bytes_accessed=2 << 20, transcendentals=0
        ),
        name="coefs",
    )(rows, mean_bank, read_bank.reshape(2, SLOTS * RANK, WIDTH))


def erased_rows(rows_ref, sum_ref, sum1_ref, sum2_ref, sum3_ref, write_ref):
    total = sum_ref[...] + sum1_ref[...].astype(F32)
    total = total + sum2_ref[...].astype(F32) + sum3_ref[...].astype(F32)
    both = jnp.concatenate([total, pltpu.roll(total, RANK, 1)], axis=0)
    wide = jnp.concatenate([both] * (SLOTS * RANK // 128), axis=1)
    wide = jnp.where(slot_mask(PACKED), wide, 0.0).astype(BF)
    delta = jnp.dot(wide, write_ref[...], preferred_element_type=F32).astype(BF)
    return rows_ref[...].astype(F32) - delta.astype(F32)


def spread_body(core_ref, rows_ref, sum_ref, sum1_ref, sum2_ref, sum3_ref, write_ref, out_ref):
    erased = erased_rows(rows_ref, sum_ref, sum1_ref, sum2_ref, sum3_ref, write_ref).astype(BF).astype(F32)
    first_core = core_ref[0] == 0
    for y in range(RING):
        start = QUARTER * 2 * (y % 2)
        low = erased[:, start : start + QUARTER]
        high = erased[:, start + QUARTER : start + 2 * QUARTER]
        part = jnp.where(first_core, low, high) if y < 2 else jnp.where(first_core, high, low)
        for z in range(RING):
            pieces = []
            for step in range(RING):
                start = PART * (z * RING + (y + step) % RING)
                pieces.append(part[start : start + PART])
            out_ref[z * RING + y] = jnp.concatenate(pieces, axis=0).astype(BF)


def home_body(rows_ref, sum_ref, sum1_ref, sum2_ref, sum3_ref, write_ref, out_ref):
    out_ref[...] = erased_rows(rows_ref, sum_ref, sum1_ref, sum2_ref, sum3_ref, write_ref).astype(BF)


def apply_eraser(body, rows, summed, others, write_bank, site, shape, extra=()):
    write_bank = write_bank.reshape(2, SLOTS * RANK, WIDTH)
    if site == 0:
        write_bank = in_hbm(write_bank)[0]
    return pl.pallas_call(
        body,
        grid=(1,),
        in_specs=[pl.BlockSpec(memory_space=pltpu.SMEM)] * len(extra)
        + [
            whole((PACKED, WIDTH)),
            *[whole((PACKED // 2, 128))] * RING,
            pl.BlockSpec((None, SLOTS * RANK, WIDTH), lambda i: (site, 0, 0)),
        ],
        out_specs=whole(shape),
        out_shape=jax.ShapeDtypeStruct(shape, BF),
        compiler_params=params(16),
        cost_estimate=pl.CostEstimate(
            flops=2 * PACKED * WIDTH * SLOTS * RANK, bytes_accessed=3 << 20, transcendentals=0
        ),
        name="erase",
    )(*extra, rows, summed, *others, write_bank)


def along_col(values, move):
    return lax.ppermute(values, "col", [(i, move(i)) for i in range(8)])


def along_y(values, step):
    return lax.ppermute(
        values, "row", [(i, i // RING * RING + (i + step) % RING) for i in range(ROWS)]
    )


def along_z(values, step):
    return lax.ppermute(values, "row", [(i, (i + RING * step) % ROWS) for i in range(ROWS)])


def gather_sums(partial, short):
    partial = partial + along_col(short, lambda i: i ^ 1).astype(F32)
    short = partial.astype(BF)
    return partial, [along_col(short, lambda i, by=by: (i + by) % COLS) for by in (2, 6, 4)]


def compact_body(*refs):
    targets, rows_ref, out_ref = refs[:RING], refs[RING], refs[RING + 1]
    rows = rows_ref[...].astype(F32)
    for step in range(RING):
        table = (
            lax.broadcasted_iota(jnp.int32, (PACKED, BLOCK), 0) == targets[step][...]
        ).astype(BF)
        part = rows[:, PART * step : PART * (step + 1), :].reshape(PACKED, QUARTER).astype(BF)
        picked = lax.dot_general(
            table, part, (((0,), (0,)), ((), ())), preferred_element_type=F32
        )
        out_ref[BLOCK * step : BLOCK * (step + 1), :] = picked.astype(BF)


def compact(targets, rows):
    return pl.pallas_call(
        compact_body,
        grid=(1,),
        in_specs=[whole((1, BLOCK))] * RING + [whole((ROWS, RING * PART, QUARTER))],
        out_specs=whole((RING * BLOCK, QUARTER)),
        out_shape=jax.ShapeDtypeStruct((RING * BLOCK, QUARTER), BF),
        compiler_params=params(16),
        cost_estimate=pl.CostEstimate(
            flops=2 * RING * BLOCK * PACKED * QUARTER, bytes_accessed=1 << 20, transcendentals=0
        ),
        name="compact",
    )(*targets, rows)


def project_body(place_ref, *refs):
    same, other = refs[0:RING], refs[RING : 2 * RING]
    kept, swapped = refs[2 * RING : 3 * RING], refs[3 * RING : 4 * RING]
    far_ref, up_ref, down_ref, own_ref, weight_ref, act_ref, sems, act_sems = refs[4 * RING :]
    x, near, z = place_ref[0], place_ref[1], place_ref[2]

    def load(step, which, block):
        source = (kept, swapped)[which][step]
        return pltpu.make_async_copy(
            source.at[pl.ds(0, QUARTER), :],
            weight_ref.at[block, pl.ds(which * QUARTER, QUARTER), :],
            sems.at[block, which],
        )

    def fetch(step, which):
        source = (same, other)[which][step]
        return pltpu.make_async_copy(source, act_ref.at[step, which], act_sems.at[step, which])

    for step, offset in enumerate(AROUND):
        for which in range(2):
            load(step, which, (z + offset) & 3).start()
            fetch(step, which).start()
    near = pl.multiple_of(near * QUARTER, QUARTER)
    away = pl.multiple_of(QUARTER - near, QUARTER)
    for tile in range(0, WIDTH, TILE):
        columns = pl.ds(tile, TILE)
        product = jnp.zeros((RING * BLOCK, TILE), F32)
        for step, offset in enumerate(AROUND):
            block = (x + offset) & 3
            if tile == 0:
                for which in range(2):
                    load(step, which, block).wait()
                    fetch(step, which).wait()
            product += jnp.dot(
                act_ref[step, 0],
                weight_ref[block, pl.ds(near, QUARTER), columns],
                preferred_element_type=F32,
            )
            product += jnp.dot(
                act_ref[step, 1],
                weight_ref[block, pl.ds(away, QUARTER), columns],
                preferred_element_type=F32,
            )
        own_ref[:, columns] = product[:BLOCK]
        up_ref[:, columns] = product[BLOCK : 2 * BLOCK].astype(BF)
        far_ref[:, columns] = product[2 * BLOCK : 3 * BLOCK].astype(BF)
        down_ref[:, columns] = product[3 * BLOCK :].astype(BF)


def project(place, same, other, kept, swapped):
    out = whole((BLOCK, WIDTH))
    sent = jax.ShapeDtypeStruct((BLOCK, WIDTH), BF)
    return pl.pallas_call(
        project_body,
        grid=(1,),
        in_specs=[pl.BlockSpec(memory_space=pltpu.SMEM)]
        + [pl.BlockSpec(memory_space=pl.ANY)] * 8
        + ([pl.BlockSpec(memory_space=pltpu.HBM)] * 3 + [pl.BlockSpec(memory_space=pl.ANY)]) * 2,
        out_specs=[out] * 4,
        out_shape=[sent, sent, sent, jax.ShapeDtypeStruct((BLOCK, WIDTH), F32)],
        scratch_shapes=[
            pltpu.VMEM((RING, 2 * QUARTER, WIDTH), BF),
            pltpu.VMEM((RING, 2, RING * BLOCK, QUARTER), BF),
            pltpu.SemaphoreType.DMA((RING, 2)),
            pltpu.SemaphoreType.DMA((RING, 2)),
        ],
        compiler_params=params(20),
        cost_estimate=pl.CostEstimate(
            flops=2 * RING * BLOCK * 8 * QUARTER * WIDTH, bytes_accessed=7 << 20, transcendentals=0
        ),
        name="project",
    )(place, *same, *other, *in_hbm(*kept[:3]), kept[3], *in_hbm(*swapped[:3]), swapped[3])


def local(
    queries,
    new_keys,
    new_values,
    key_cache,
    value_cache,
    residual,
    out_weight,
    tenant,
    tenant_slot_index,
    read_bank,
    write_bank,
    mean_bank,
):
    row, col = lax.axis_index("row"), lax.axis_index("col")
    x, core, y, z = col >> 1, col & 1, row & 3, row >> 2
    half = out_weight.shape[0] // 2
    kept0 = out_weight[:half]
    swapped0 = lax.ppermute(out_weight[half:], "row", [(i, i ^ 2) for i in range(ROWS)])
    kept1, kept2 = along_z(kept0, 1), along_z(kept0, 3)
    target = packed_position(tenant, tenant_slot_index)

    def dispatch(packed):
        packed = packed.reshape(ROWS, PART, WIDTH)
        return lax.all_to_all(packed, "row", 0, 0, tiled=True).reshape(PACKED, WIDTH)

    packed, target = attend_and_pack(
        queries, new_keys, new_values, key_cache, value_cache, target[None]
    )
    targets = [target] + [along_y(target, by) for by in (3, 2, 1)]
    swapped0, kept1, kept2, packed = lax.optimization_barrier((swapped0, kept1, kept2, packed))
    rows = dispatch(packed)
    table = (jnp.arange(PACKED, dtype=jnp.int32)[:, None] == target).astype(BF)
    partial, short = partial_coefs(rows, mean_bank, read_bank, 0)
    swapped0, short = lax.optimization_barrier((swapped0, short))
    swapped1, swapped2 = along_z(swapped0, 1), along_z(swapped0, 3)
    summed, others = gather_sums(partial, short)
    shape = (ROWS, RING * PART, QUARTER)
    cleaned = apply_eraser(spread_body, rows, summed, others, write_bank, 0, shape, (core[None],))
    swapped1, swapped2, cleaned = lax.optimization_barrier((swapped1, swapped2, cleaned))
    cleaned = lax.all_to_all(cleaned, "row", 0, 0, tiled=True)
    kept1, swapped2, cleaned = lax.optimization_barrier((kept1, swapped2, cleaned))
    kept3, swapped3 = along_z(kept1, 1), along_z(swapped2, 3)
    here = compact(targets, cleaned)

    after = along_col(here, lambda i: (i + 2) % 8)
    before = along_col(here, lambda i: (i - 2) % 8)
    across = along_col(here, lambda i: (i + 4) % 8)
    same = [here, after, before, across]
    other = [along_col(part, lambda i: i ^ 1) for part in same]
    place = jnp.stack([x, core ^ (y >> 1), z])
    kept, swapped = [out_weight, kept1, kept2, kept3], [swapped0, swapped1, swapped2, swapped3]
    far, up, down, own = project(place, same, other, kept, swapped)
    far, up, down = along_y(far, 2), along_y(up, 1), along_y(down, 3)
    projected = own + up.astype(F32) + down.astype(F32) + far.astype(F32)
    hidden = (residual.astype(F32) + projected).astype(BF)

    rows = dispatch(jnp.dot(table, hidden, preferred_element_type=F32).astype(BF))
    summed, others = gather_sums(*partial_coefs(rows, mean_bank, read_bank, 1))
    erased = apply_eraser(home_body, rows, summed, others, write_bank, 1, (PACKED, WIDTH))
    erased = lax.all_to_all(erased.reshape(ROWS, PART, WIDTH), "row", 0, 0, tiled=True)
    return lax.dot_general(
        table,
        erased.reshape(PACKED, WIDTH),
        (((0,), (0,)), ((), ())),
        preferred_element_type=F32,
    ).astype(BF)


def solution(mesh):
    return jax.shard_map(
        local,
        mesh=mesh,
        in_specs=(
            P("row", "col"),
            P("row", "col"),
            P("row", "col"),
            P("row", None, "col"),
            P("row", None, "col"),
            P("row", "col"),
            P("row", "col"),
            P("row"),
            P(),
            P(None, "row", None, "col"),
            P(None, "row", None, "col"),
            P(None, "row", "col"),
        ),
        out_specs=P("row", "col"),
        check_vma=False,
    )
```

```python
import functools
import math

import jax
import jax.numpy as jnp
from jax import lax
from jax.experimental import pallas as pl
from jax.experimental.pallas import tpu as pltpu
from jax.sharding import PartitionSpec as P

HEADS = 64
KVH = 8
HD = 128
MOST = 3
ROWS = 16
COLS = 8
RING = 4
AROUND = (0, 3, 1, 2)
SLOTS = 8
RANK = 64
PART = SLOTS * MOST
PACKED = ROWS * PART
BLOCK = 128
TILE = 1024
CHUNK = 32
WIDTH = 1024
QUARTER = WIDTH // RING

BF = jnp.bfloat16
F32 = jnp.float32


def whole(shape):
    return pl.BlockSpec(shape, lambda *_: (0,) * len(shape))


def params(mib):
    return pltpu.CompilerParams(vmem_limit_bytes=mib << 20)


def in_hbm(*arrays):
    return [pltpu.with_memory_space_constraint(array, pltpu.HBM) for array in arrays]


def attend_body(
    q_ref, key_ref, value_ref, target_ref, keys_ref, values_ref,
    out_ref, after_ref, heads_ref, mix_ref, all_ref
):
    step = pl.program_id(0)
    group = HEADS // KVH
    scale = 1.0 / math.sqrt(HD)
    q = q_ref[...].astype(F32)
    for head in range(group):
        heads_ref[pl.ds(head, CHUNK, stride=group), :] = q[:, HD * head : HD * (head + 1)]
    heads = heads_ref[...].reshape(CHUNK, group, HD)
    past = scale * jnp.einsum(
        "bhd,bld->bhl", heads.astype(BF), keys_ref[...], preferred_element_type=F32
    )
    key = key_ref[...].astype(F32)[:, None, :]
    own = scale * jnp.sum(heads * key, axis=-1, keepdims=True)
    top = jnp.maximum(jnp.max(past, axis=-1, keepdims=True), own)
    past, own = jnp.exp(past - top), jnp.exp(own - top)
    inverse = 1.0 / (jnp.sum(past, axis=-1, keepdims=True) + own)
    weights = (past * inverse).astype(BF)
    own = (own * inverse).astype(BF).astype(F32)
    mixed = jnp.einsum("bhl,bld->bhd", weights, values_ref[...], preferred_element_type=F32)
    mixed = mixed + own * value_ref[...].astype(F32)[:, None, :]
    mix_ref[...] = mixed.reshape(CHUNK * group, HD)
    rows = pl.ds(pl.multiple_of(step * CHUNK, CHUNK), CHUNK)
    for head in range(group):
        picked = mix_ref[pl.ds(head, CHUNK, stride=group), :]
        all_ref[rows, HD * head : HD * (head + 1)] = picked.astype(BF)

    @pl.when(step == pl.num_programs(0) - 1)
    def _():
        table = (
            lax.broadcasted_iota(jnp.int32, (PACKED, BLOCK), 0) == target_ref[...]
        ).astype(BF)
        packed = jnp.dot(table, all_ref[...], preferred_element_type=F32)
        out_ref[...] = packed.astype(BF)
        after_ref[...] = target_ref[...]


def attend_and_pack(queries, new_keys, new_values, key_cache, value_cache, target):
    history = key_cache.shape[1]
    group = HEADS // KVH
    by_row = lambda *tail: pl.BlockSpec((CHUNK,) + tail, lambda i: (i,) + (0,) * len(tail))
    queries, new_keys, new_values, key_cache, value_cache = in_hbm(
        queries, new_keys, new_values, key_cache, value_cache
    )
    return pl.pallas_call(
        attend_body,
        grid=(BLOCK // CHUNK,),
        in_specs=[
            by_row(WIDTH),
            by_row(HD),
            by_row(HD),
            whole((1, BLOCK)),
            by_row(history, HD),
            by_row(history, HD),
        ],
        out_specs=[whole((PACKED, WIDTH)), whole((1, BLOCK))],
        out_shape=[
            jax.ShapeDtypeStruct((PACKED, WIDTH), BF),
            jax.ShapeDtypeStruct((1, BLOCK), jnp.int32),
        ],
        scratch_shapes=[
            pltpu.VMEM((CHUNK * group, HD), F32),
            pltpu.VMEM((CHUNK * group, HD), F32),
            pltpu.VMEM((BLOCK, WIDTH), BF),
        ],
        compiler_params=params(20),
        cost_estimate=pl.CostEstimate(
            flops=4 * BLOCK * history * WIDTH, bytes_accessed=17 << 20, transcendentals=0
        ),
        name="attend",
    )(queries, new_keys, new_values, target, key_cache, value_cache)


def packed_position(tenant, tenant_slot_index):
    tenants = jnp.arange(tenant_slot_index.shape[0], dtype=jnp.int32)
    slot = jnp.sum(
        jnp.where(tenant[:, None] == tenants[None, :], tenant_slot_index[None, :], 0), axis=1
    )
    order = jnp.arange(tenant.shape[0], dtype=jnp.int32)
    earlier = (tenant[:, None] == tenant[None, :]) & (order[None, :] < order[:, None])
    rank = jnp.sum(earlier.astype(jnp.int32), axis=1)
    return slot // SLOTS * PART + rank * SLOTS + slot % SLOTS


def slot_mask(rows):
    shape = (rows, SLOTS * RANK)
    return lax.broadcasted_iota(jnp.int32, shape, 0) % SLOTS == (
        lax.broadcasted_iota(jnp.int32, shape, 1) // RANK
    )


def coef_body(rows_ref, mean_ref, read_ref, out_ref, short_ref):
    rows = rows_ref[...].astype(F32).reshape(PACKED // SLOTS, SLOTS, WIDTH)
    centered = (rows - mean_ref[...].astype(F32)).astype(BF).reshape(PACKED, WIDTH)
    full = lax.dot_general(
        centered, read_ref[...], (((1,), (1,)), ((), ())), preferred_element_type=F32
    )
    full = jnp.where(slot_mask(PACKED), full, 0.0)
    lanes = full[:, :128] + full[:, 128:256] + full[:, 256:384] + full[:, 384:]
    half = PACKED // 2
    packed = lanes[:half] + pltpu.roll(lanes[half:], RANK, 1)
    out_ref[...] = packed
    short_ref[...] = packed.astype(BF)


def partial_coefs(rows, mean_bank, read_bank, site):
    return pl.pallas_call(
        coef_body,
        grid=(1,),
        in_specs=[
            whole((PACKED, WIDTH)),
            pl.BlockSpec((None, SLOTS, WIDTH), lambda i: (site, 0, 0)),
            pl.BlockSpec((None, SLOTS * RANK, WIDTH), lambda i: (site, 0, 0)),
        ],
        out_specs=[whole((PACKED // 2, 128))] * 2,
        out_shape=[jax.ShapeDtypeStruct((PACKED // 2, 128), kind) for kind in (F32, BF)],
        compiler_params=params(16),
        cost_estimate=pl.CostEstimate(
            flops=2 * PACKED * WIDTH * SLOTS * RANK, bytes_accessed=2 << 20, transcendentals=0
        ),
        name="coefs",
    )(rows, mean_bank, read_bank.reshape(2, SLOTS * RANK, WIDTH))


def erased_rows(rows_ref, sum_ref, sum1_ref, sum2_ref, sum3_ref, write_ref):
    total = sum_ref[...] + sum1_ref[...].astype(F32)
    total = total + sum2_ref[...].astype(F32) + sum3_ref[...].astype(F32)
    both = jnp.concatenate([total, pltpu.roll(total, RANK, 1)], axis=0)
    wide = jnp.concatenate([both] * (SLOTS * RANK // 128), axis=1)
    wide = jnp.where(slot_mask(PACKED), wide, 0.0).astype(BF)
    delta = jnp.dot(wide, write_ref[...], preferred_element_type=F32).astype(BF)
    return rows_ref[...].astype(F32) - delta.astype(F32)


def spread_body(core_ref, rows_ref, sum_ref, sum1_ref, sum2_ref, sum3_ref, write_ref, out_ref):
    erased = erased_rows(rows_ref, sum_ref, sum1_ref, sum2_ref, sum3_ref, write_ref).astype(BF).astype(F32)
    first_core = core_ref[0] == 0
    for y in range(RING):
        start = QUARTER * 2 * (y % 2)
        low = erased[:, start : start + QUARTER]
        high = erased[:, start + QUARTER : start + 2 * QUARTER]
        part = jnp.where(first_core, low, high) if y < 2 else jnp.where(first_core, high, low)
        for z in range(RING):
            pieces = []
            for step in range(RING):
                start = PART * (z * RING + (y + step) % RING)
                pieces.append(part[start : start + PART])
            out_ref[z * RING + y] = jnp.concatenate(pieces, axis=0).astype(BF)


def home_body(rows_ref, sum_ref, sum1_ref, sum2_ref, sum3_ref, write_ref, out_ref):
    out_ref[...] = erased_rows(rows_ref, sum_ref, sum1_ref, sum2_ref, sum3_ref, write_ref).astype(BF)


def apply_eraser(body, rows, summed, others, write_bank, site, shape, extra=()):
    write_bank = write_bank.reshape(2, SLOTS * RANK, WIDTH)
    if site == 0:
        write_bank = in_hbm(write_bank)[0]
    return pl.pallas_call(
        body,
        grid=(1,),
        in_specs=[pl.BlockSpec(memory_space=pltpu.SMEM)] * len(extra)
        + [
            whole((PACKED, WIDTH)),
            *[whole((PACKED // 2, 128))] * RING,
            pl.BlockSpec((None, SLOTS * RANK, WIDTH), lambda i: (site, 0, 0)),
        ],
        out_specs=whole(shape),
        out_shape=jax.ShapeDtypeStruct(shape, BF),
        compiler_params=params(16),
        cost_estimate=pl.CostEstimate(
            flops=2 * PACKED * WIDTH * SLOTS * RANK, bytes_accessed=3 << 20, transcendentals=0
        ),
        name="erase",
    )(*extra, rows, summed, *others, write_bank)


def along_col(values, move):
    return lax.ppermute(values, "col", [(i, move(i)) for i in range(8)])


def along_y(values, step):
    return lax.ppermute(
        values, "row", [(i, i // RING * RING + (i + step) % RING) for i in range(ROWS)]
    )


def along_z(values, step):
    return lax.ppermute(values, "row", [(i, (i + RING * step) % ROWS) for i in range(ROWS)])


def gather_sums(partial, short):
    partial = partial + along_col(short, lambda i: i ^ 1).astype(F32)
    short = partial.astype(BF)
    return partial, [along_col(short, lambda i, by=by: (i + by) % COLS) for by in (2, 6, 4)]


def compact_body(*refs):
    targets, rows_ref, out_ref = refs[:RING], refs[RING], refs[RING + 1]
    rows = rows_ref[...].astype(F32)
    for step in range(RING):
        table = (
            lax.broadcasted_iota(jnp.int32, (PACKED, BLOCK), 0) == targets[step][...]
        ).astype(BF)
        part = rows[:, PART * step : PART * (step + 1), :].reshape(PACKED, QUARTER).astype(BF)
        picked = lax.dot_general(
            table, part, (((0,), (0,)), ((), ())), preferred_element_type=F32
        )
        out_ref[BLOCK * step : BLOCK * (step + 1), :] = picked.astype(BF)


def compact(targets, rows):
    return pl.pallas_call(
        compact_body,
        grid=(1,),
        in_specs=[whole((1, BLOCK))] * RING + [whole((ROWS, RING * PART, QUARTER))],
        out_specs=whole((RING * BLOCK, QUARTER)),
        out_shape=jax.ShapeDtypeStruct((RING * BLOCK, QUARTER), BF),
        compiler_params=params(16),
        cost_estimate=pl.CostEstimate(
            flops=2 * RING * BLOCK * PACKED * QUARTER, bytes_accessed=1 << 20, transcendentals=0
        ),
        name="compact",
    )(*targets, rows)


def project_body(place_ref, *refs):
    same, other = refs[0:RING], refs[RING : 2 * RING]
    kept, swapped = refs[2 * RING : 3 * RING], refs[3 * RING : 4 * RING]
    far_ref, up_ref, down_ref, own_ref, weight_ref, act_ref, sems, act_sems = refs[4 * RING :]
    x, near, z = place_ref[0], place_ref[1], place_ref[2]

    def load(step, which, block):
        source = (kept, swapped)[which][step]
        return pltpu.make_async_copy(
            source.at[pl.ds(0, QUARTER), :],
            weight_ref.at[block, pl.ds(which * QUARTER, QUARTER), :],
            sems.at[block, which],
        )

    def fetch(step, which):
        source = (same, other)[which][step]
        return pltpu.make_async_copy(source, act_ref.at[step, which], act_sems.at[step, which])

    for step, offset in enumerate(AROUND):
        for which in range(2):
            load(step, which, (z + offset) & 3).start()
            fetch(step, which).start()
    near = pl.multiple_of(near * QUARTER, QUARTER)
    away = pl.multiple_of(QUARTER - near, QUARTER)
    for tile in range(0, WIDTH, TILE):
        columns = pl.ds(tile, TILE)
        product = jnp.zeros((RING * BLOCK, TILE), F32)
        for step, offset in enumerate(AROUND):
            block = (x + offset) & 3
            if tile == 0:
                for which in range(2):
                    load(step, which, block).wait()
                    fetch(step, which).wait()
            product += jnp.dot(
                act_ref[step, 0],
                weight_ref[block, pl.ds(near, QUARTER), columns],
                preferred_element_type=F32,
            )
            product += jnp.dot(
                act_ref[step, 1],
                weight_ref[block, pl.ds(away, QUARTER), columns],
                preferred_element_type=F32,
            )
        own_ref[:, columns] = product[:BLOCK]
        up_ref[:, columns] = product[BLOCK : 2 * BLOCK].astype(BF)
        far_ref[:, columns] = product[2 * BLOCK : 3 * BLOCK].astype(BF)
        down_ref[:, columns] = product[3 * BLOCK :].astype(BF)


def project(place, same, other, kept, swapped):
    out = whole((BLOCK, WIDTH))
    sent = jax.ShapeDtypeStruct((BLOCK, WIDTH), BF)
    return pl.pallas_call(
        project_body,
        grid=(1,),
        in_specs=[pl.BlockSpec(memory_space=pltpu.SMEM)]
        + [pl.BlockSpec(memory_space=pl.ANY)] * 8
        + ([pl.BlockSpec(memory_space=pltpu.HBM)] * 3 + [pl.BlockSpec(memory_space=pl.ANY)]) * 2,
        out_specs=[out] * 4,
        out_shape=[sent, sent, sent, jax.ShapeDtypeStruct((BLOCK, WIDTH), F32)],
        scratch_shapes=[
            pltpu.VMEM((RING, 2 * QUARTER, WIDTH), BF),
            pltpu.VMEM((RING, 2, RING * BLOCK, QUARTER), BF),
            pltpu.SemaphoreType.DMA((RING, 2)),
            pltpu.SemaphoreType.DMA((RING, 2)),
        ],
        compiler_params=params(20),
        cost_estimate=pl.CostEstimate(
            flops=2 * RING * BLOCK * 8 * QUARTER * WIDTH, bytes_accessed=7 << 20, transcendentals=0
        ),
        name="project",
    )(place, *same, *other, *in_hbm(*kept[:3]), kept[3], *in_hbm(*swapped[:3]), swapped[3])


def local(
    queries,
    new_keys,
    new_values,
    key_cache,
    value_cache,
    residual,
    out_weight,
    tenant,
    tenant_slot_index,
    read_bank,
    write_bank,
    mean_bank,
):
    row, col = lax.axis_index("row"), lax.axis_index("col")
    x, core, y, z = col >> 1, col & 1, row & 3, row >> 2
    half = out_weight.shape[0] // 2
    kept0 = out_weight[:half]
    swapped0 = lax.ppermute(out_weight[half:], "row", [(i, i ^ 2) for i in range(ROWS)])
    kept1, kept2 = along_z(kept0, 1), along_z(kept0, 3)
    target = packed_position(tenant, tenant_slot_index)

    def dispatch(packed):
        packed = packed.reshape(ROWS, PART, WIDTH)
        return lax.all_to_all(packed, "row", 0, 0, tiled=True).reshape(PACKED, WIDTH)

    packed, target = attend_and_pack(
        queries, new_keys, new_values, key_cache, value_cache, target[None]
    )
    targets = [target] + [along_y(target, by) for by in (3, 2, 1)]
    swapped0, kept1, kept2, packed = lax.optimization_barrier((swapped0, kept1, kept2, packed))
    rows = dispatch(packed)
    table = (jnp.arange(PACKED, dtype=jnp.int32)[:, None] == target).astype(BF)
    partial, short = partial_coefs(rows, mean_bank, read_bank, 0)
    swapped0, short = lax.optimization_barrier((swapped0, short))
    swapped1, swapped2 = along_z(swapped0, 1), along_z(swapped0, 3)
    summed, others = gather_sums(partial, short)
    shape = (ROWS, RING * PART, QUARTER)
    cleaned = apply_eraser(spread_body, rows, summed, others, write_bank, 0, shape, (core[None],))
    swapped1, swapped2, cleaned = lax.optimization_barrier((swapped1, swapped2, cleaned))
    cleaned = lax.all_to_all(cleaned, "row", 0, 0, tiled=True)
    kept1, swapped2, cleaned = lax.optimization_barrier((kept1, swapped2, cleaned))
    kept3, swapped3 = along_z(kept1, 1), along_z(swapped2, 3)
    here = compact(targets, cleaned)

    after = along_col(here, lambda i: (i + 2) % 8)
    before = along_col(here, lambda i: (i - 2) % 8)
    across = along_col(here, lambda i: (i + 4) % 8)
    same = [here, after, before, across]
    other = [along_col(part, lambda i: i ^ 1) for part in same]
    place = jnp.stack([x, core ^ (y >> 1), z])
    kept, swapped = [out_weight, kept1, kept2, kept3], [swapped0, swapped1, swapped2, swapped3]
    far, up, down, own = project(place, same, other, kept, swapped)
    far, up, down = along_y(far, 2), along_y(up, 1), along_y(down, 3)
    projected = own + up.astype(F32) + down.astype(F32) + far.astype(F32)
    hidden = (residual.astype(F32) + projected).astype(BF)

    rows = dispatch(jnp.dot(table, hidden, preferred_element_type=F32).astype(BF))
    summed, others = gather_sums(*partial_coefs(rows, mean_bank, read_bank, 1))
    erased = apply_eraser(home_body, rows, summed, others, write_bank, 1, (PACKED, WIDTH))
    erased = lax.all_to_all(erased.reshape(ROWS, PART, WIDTH), "row", 0, 0, tiled=True)
    return lax.dot_general(
        table,
        erased.reshape(PACKED, WIDTH),
        (((0,), (0,)), ((), ())),
        preferred_element_type=F32,
    ).astype(BF)


def solution(mesh):
    return jax.shard_map(
        local,
        mesh=mesh,
        in_specs=(
            P("row", "col"),
            P("row", "col"),
            P("row", "col"),
            P("row", None, "col"),
            P("row", None, "col"),
            P("row", "col"),
            P("row", "col"),
            P("row"),
            P(),
            P(None, "row", None, "col"),
            P(None, "row", None, "col"),
            P(None, "row", "col"),
        ),
        out_specs=P("row", "col"),
        check_vma=False,
    )
```
